32 devices in a mesh: seq: 4 (over y, core), fsdp: 8 (over z, x).
Axes of the slice: x: 2, y: 2, z: 4, core: 2. Of those that a mesh axis runs over, the one named last changes fastest.
Arguments:
- layer_input: bfloat16 [8, 2048, 1024], P('fsdp', 'seq'), may hold values from -19 to 19
- w_qkv: bfloat16 [1024, 3072], P(('seq', 'fsdp')), may hold values from -0.1875 to 0.1875
- w_out: bfloat16 [1024, 1024], P(('seq', 'fsdp')), may hold values from -1 to 1
- w_up: bfloat16 [1024, 4096], P(('seq', 'fsdp')), may hold values from -0.1875 to 0.1875
- w_down: bfloat16 [4096, 1024], P(('seq', 'fsdp')), may hold values from -0.09375 to 0.09375
- gain_attn: bfloat16 [1024], P(('seq', 'fsdp')), may hold values from 0.099609375 to 1.8984375
- gain_mlp: bfloat16 [1024], P(('seq', 'fsdp')), may hold values from 0.099609375 to 1.8984375
- out_grad: bfloat16 [8, 2048, 1024], P('fsdp', 'seq'), may hold values from -6 to 6
- moment_qkv: float32 [1024, 3072], P(('seq', 'fsdp')), may hold values from -40 to 40
- square_qkv: float32 [1024, 3072], P(('seq', 'fsdp')), may hold values from 108.1344 to 434.176
- moment_out: float32 [1024, 1024], P(('seq', 'fsdp')), may hold values from -6 to 6
- square_out: float32 [1024, 1024], P(('seq', 'fsdp')), may hold values from 2.78528 to 11.14112
- moment_up: float32 [1024, 4096], P(('seq', 'fsdp')), may hold values from -32 to 32
- square_up: float32 [1024, 4096], P(('seq', 'fsdp')), may hold values from 52.4288 to 212.992
- moment_down: float32 [4096, 1024], P(('seq', 'fsdp')), may hold values from -48 to 48
- square_down: float32 [4096, 1024], P(('seq', 'fsdp')), may hold values from 155.648 to 622.592
- moment_gattn: float32 [1024], P(('seq', 'fsdp')), may hold values from -80 to 80
- square_gattn: float32 [1024], P(('seq', 'fsdp')), may hold values from 434.176 to 1736.704
- moment_gmlp: float32 [1024], P(('seq', 'fsdp')), may hold values from -64 to 64
- square_gmlp: float32 [1024], P(('seq', 'fsdp')), may hold values from 212.992 to 851.968
Outputs:
- layer_output: bfloat16 [8, 2048, 1024], P('fsdp', 'seq')
- input_grad: bfloat16 [8, 2048, 1024], P('fsdp', 'seq')
- grad_qkv: float32 [1024, 3072], P(('seq', 'fsdp'))
- grad_out: float32 [1024, 1024], P(('seq', 'fsdp'))
- grad_up: float32 [1024, 4096], P(('seq', 'fsdp'))
- grad_down: float32 [4096, 1024], P(('seq', 'fsdp'))
- grad_gattn: float32 [1024], P(('seq', 'fsdp'))
- grad_gmlp: float32 [1024], P(('seq', 'fsdp'))
- next_moment_qkv: float32 [1024, 3072], P(('seq', 'fsdp'))
- next_moment_out: float32 [1024, 1024], P(('seq', 'fsdp'))
- next_moment_up: float32 [1024, 4096], P(('seq', 'fsdp'))
- next_moment_down: float32 [4096, 1024], P(('seq', 'fsdp'))
- next_moment_gattn: float32 [1024], P(('seq', 'fsdp'))
- next_moment_gmlp: float32 [1024], P(('seq', 'fsdp'))
- next_square_qkv: float32 [1024, 3072], P(('seq', 'fsdp'))
- next_square_out: float32 [1024, 1024], P(('seq', 'fsdp'))
- next_square_up: float32 [1024, 4096], P(('seq', 'fsdp'))
- next_square_down: float32 [4096, 1024], P(('seq', 'fsdp'))
- next_square_gattn: float32 [1024], P(('seq', 'fsdp'))
- next_square_gmlp: float32 [1024], P(('seq', 'fsdp'))
- change_qkv: float32 [1024, 3072], P(('seq', 'fsdp'))
- change_out: float32 [1024, 1024], P(('seq', 'fsdp'))
- change_up: float32 [1024, 4096], P(('seq', 'fsdp'))
- change_down: float32 [4096, 1024], P(('seq', 'fsdp'))
- change_gattn: float32 [1024], P(('seq', 'fsdp'))
- change_gmlp: float32 [1024], P(('seq', 'fsdp'))
The draws below stay inside these ranges and needn't reach their ends.
All inputs are finite; a program needn't handle non-finite values.
Results may differ from the reference program's by a relative error of at most 0.0089.
Values may be sent and summed in bfloat16 or wider, within the bound.
No kernel may reach another device: no remote copies, remote signals or barrier semaphores. Data moves between devices by JAX's collectives and lax.ppermute only.
A program may use at most 192 MiB of HBM per device.

```python
import math
import jax
import jax.numpy as jnp
from jax import lax

D = 1024
HEADS = 16
HD = 64
FF = 4096
ROT = 16
STEP = 10
LENGTH = 2048
SEQS = 8
TOKENS = 16384


def draw_layer_input(key, part):
    streams = jax.random.split(jax.random.fold_in(key, 11), 4)
    shape = (SEQS, LENGTH, D)
    base = jnp.clip(jax.random.normal(streams[0], shape, jnp.float32), -6.0, 6.0)
    row_scale = jnp.exp(jax.random.uniform(streams[1], (SEQS, LENGTH, 1), jnp.float32, -1.15, 1.15))
    col_scale = jnp.exp(jax.random.uniform(streams[2], (1, 1, D), jnp.float32, -0.6, 0.6))
    shifted = jax.random.uniform(streams[3], (SEQS, LENGTH, 1), jnp.float32, -1.0, 1.0)
    return (0.5 * base * row_scale * col_scale + shifted).astype(jnp.bfloat16)


def shard_levels(own_key, shape, cuts, low, high):
    def one(axis_at, blocks):
        draws = jax.random.uniform(jax.random.fold_in(jax.random.fold_in(own_key, 6), axis_at), (blocks,), jnp.float32, low / len(cuts), high / len(cuts))
        return jnp.repeat(jnp.exp(draws), shape[axis_at] // blocks).reshape((-1,) + (1,) * (len(shape) - axis_at - 1))

    factor_of = one(*cuts[0])
    for cut in cuts[1:]:
        factor_of = factor_of * one(*cut)
    return factor_of


def noise(key, dims, width, bound, pieces=(), held_as=jnp.bfloat16):
    entries = jax.random.normal(key, dims, jnp.float32) * width
    if len(pieces) > 0:
        entries = shard_levels(key, dims, pieces, -0.22, 0.18) * entries
    return jnp.clip(entries, min=-bound, max=bound).astype(held_as)


def setup_inputs(seed: int = 0) -> dict:
    key_of = jax.random.split(jax.random.key(seed), 21)
    return {
        "layer_input": draw_layer_input(jax.random.fold_in(key_of[20], 71), 0),
        "w_qkv": noise(key_of[1], (D, 3 * D), D ** -0.5, 0.1875, ((0, 32),)),
        "w_out": noise(key_of[2], (D, D), (D // 32) ** -0.5, 1.0, ((0, 32),)),
        "w_up": noise(key_of[3], (D, FF), D ** -0.5, 0.1875, ((0, 32),)),
        "w_down": noise(key_of[4], (FF, D), FF ** -0.5, 0.09375, ((0, 32),)),
        "gain_attn": jnp.clip(1.0 + 0.18 * jax.random.normal(key_of[5], (D,), jnp.float32), 0.099609375, 1.8984375).astype(jnp.bfloat16),
        "gain_mlp": jnp.clip(1.0 + 0.18 * jax.random.normal(key_of[6], (D,), jnp.float32), 0.099609375, 1.8984375).astype(jnp.bfloat16),
        "out_grad": noise(key_of[7], (SEQS, LENGTH, D), 1.0, 6.0, ((0, 8), (1, 4))),
        "moment_qkv": noise(key_of[8], (D, 3 * D), (0.055 * TOKENS ** 0.5), 40.0, ((0, 32),), jnp.float32),
        "square_qkv": jnp.clip(jnp.exp(math.log(434.176) - 1.3900751 * jax.random.uniform(key_of[9], (D, 3 * D), jnp.float32) ** shard_levels(key_of[9], (D, 3 * D), ((0, 32),), -0.2, 0.2)), 108.1344, 434.176),
        "moment_out": noise(key_of[10], (D, D), (0.0088 * TOKENS ** 0.5), 6.0, ((0, 32),), jnp.float32),
        "square_out": jnp.clip(jnp.exp(math.log(11.14112) - 1.3862944 * jax.random.uniform(key_of[11], (D, D), jnp.float32) ** shard_levels(key_of[11], (D, D), ((0, 32),), -0.2, 0.2)), 2.78528, 11.14112),
        "moment_up": noise(key_of[12], (D, FF), (0.0385 * TOKENS ** 0.5), 32.0, ((0, 32),), jnp.float32),
        "square_up": jnp.clip(jnp.exp(math.log(212.992) - 1.4017986 * jax.random.uniform(key_of[13], (D, FF), jnp.float32) ** shard_levels(key_of[13], (D, FF), ((0, 32),), -0.2, 0.2)), 52.4288, 212.992),
        "moment_down": noise(key_of[14], (FF, D), (0.066 * TOKENS ** 0.5), 48.0, ((0, 32),), jnp.float32),
        "square_down": jnp.clip(jnp.exp(math.log(622.592) - 1.3862944 * jax.random.uniform(key_of[15], (FF, D), jnp.float32) ** shard_levels(key_of[15], (FF, D), ((0, 32),), -0.2, 0.2)), 155.648, 622.592),
        "moment_gattn": noise(key_of[16], (D,), (0.11 * TOKENS ** 0.5), 80.0, ((0, 32),), jnp.float32),
        "square_gattn": jnp.clip(jnp.exp(math.log(1736.704) - 1.3862944 * jax.random.uniform(key_of[17], (D,), jnp.float32) ** shard_levels(key_of[17], (D,), ((0, 32),), -0.2, 0.2)), 434.176, 1736.704),
        "moment_gmlp": noise(key_of[18], (D,), (0.077 * TOKENS ** 0.5), 64.0, ((0, 32),), jnp.float32),
        "square_gmlp": jnp.clip(jnp.exp(math.log(851.968) - 1.3862944 * jax.random.uniform(key_of[19], (D,), jnp.float32) ** shard_levels(key_of[19], (D,), ((0, 32),), -0.2, 0.2)), 212.992, 851.968),
    }


@jax.custom_vjp
def low(v):
    return lax.optimization_barrier(v.astype(jnp.bfloat16)).astype(jnp.float32)

@jax.custom_vjp
def low_back(v):
    return v

def low_keep(v):
    return (low(v), None)

def low_pass(kept, grad):
    return (grad,)

def back_keep(v):
    return (v, None)

def back_low(kept, grad):
    return (low(grad),)
low.defvjp(low_keep, low_pass)
low_back.defvjp(back_keep, back_low)
EPS_NORM = 1e-05
BETA_ONE = 0.9
BETA_TWO = 0.95
RATE = 0.02
DECAY = 0.1
ADAM_EPS = 1e-08
HIGH = lax.Precision.HIGHEST

def layer_norm(row_values, gain):
    centred = row_values - lax.optimization_barrier(jnp.mean(row_values, axis=-1, keepdims=True))
    spread = lax.optimization_barrier(jnp.mean(centred * centred, axis=-1, keepdims=True))
    return centred * lax.rsqrt(spread + EPS_NORM) * gain

def rotary_tables(positions):
    half_width = ROT // 2
    frequency = 10000.0 ** (-(jnp.arange(half_width).astype(jnp.float32) * 2.0) / ROT)
    angles = positions.astype(jnp.float32)[:, None] * frequency[None, :]
    angles = jnp.concatenate([angles, angles], axis=1)
    return (jnp.cos(angles), jnp.sin(angles))

def rotate(head_values, cosine, sine_table):
    half_width = ROT // 2
    leading = head_values[..., :ROT]
    turned = jnp.concatenate([-leading[..., half_width:], leading[..., :half_width]], axis=-1)
    rotated = leading * cosine[:, None, :] + turned * sine_table[:, None, :]
    return jnp.concatenate([rotated, head_values[..., ROT:]], axis=-1)

def attend_block(query_block, key_heads, value_heads, first_row):
    scale = HD ** (-0.5)
    projected = jnp.einsum('qhd,khd->hqk', query_block, key_heads, precision=HIGH)
    scores = low_back(projected) * scale
    row_index = first_row + jnp.arange(query_block.shape[0]).astype(jnp.int32)
    col_index = jnp.arange(key_heads.shape[0]).astype(jnp.int32)
    scores = jnp.where(col_index[None, None, :] <= row_index[None, :, None], scores, -1e+30)
    row_top = lax.optimization_barrier(jnp.max(scores, axis=-1, keepdims=True))
    exponent = jnp.exp(scores - row_top)
    probability = low(exponent / lax.optimization_barrier(jnp.sum(exponent, axis=-1, keepdims=True)))
    return jnp.einsum('hqk,khd->qhd', probability, value_heads, precision=HIGH)

def one_sequence(weights, row_values):
    full_qkv, full_out, full_up, full_down, gain_first, gain_second = weights
    normed_attn = low(layer_norm(row_values, gain_first))
    normed_mlp = low(layer_norm(row_values, gain_second))
    projected = jnp.dot(normed_attn, full_qkv, precision=HIGH, preferred_element_type=jnp.float32)
    projected = low_back(projected).reshape(LENGTH, 3, HEADS, HD)
    cosine, sine_table = rotary_tables(jnp.arange(LENGTH).astype(jnp.int32))
    queries = low(rotate(projected[:, 0], cosine, sine_table))
    key_heads = low(rotate(projected[:, 1], cosine, sine_table))
    value_heads = low(projected[:, 2])
    block_rows = min(512, LENGTH)
    block_count = LENGTH // block_rows
    starts = jnp.arange(block_count).astype(jnp.int32) * block_rows
    blocks = queries.reshape(block_count, block_rows, HEADS, HD)
    attend = jax.checkpoint(lambda block_item: attend_block(block_item[0], key_heads, value_heads, block_item[1]))
    context = lax.map(attend, (blocks, starts)).reshape(LENGTH, HEADS * HD)
    context = low(low_back(context))
    attention = jnp.dot(context, full_out, precision=HIGH, preferred_element_type=jnp.float32)
    hidden = low_back(jnp.dot(normed_mlp, full_up, precision=HIGH, preferred_element_type=jnp.float32))
    activated = low(jax.nn.gelu(hidden, approximate=False))
    feed_out = jnp.dot(activated, full_down, precision=HIGH, preferred_element_type=jnp.float32)
    return row_values + attention + feed_out

def adam_step(weight, gradient, moment, square, decay_rate):
    moment_next = BETA_ONE * moment + (1.0 - BETA_ONE) * gradient
    square_next = BETA_TWO * square + (1.0 - BETA_TWO) * gradient * gradient
    moment_hat = moment_next / (1.0 - BETA_ONE ** STEP)
    square_hat = square_next / (1.0 - BETA_TWO ** STEP)
    change = -RATE * (moment_hat / (jnp.sqrt(square_hat) + ADAM_EPS) + decay_rate * weight)
    return (moment_next, square_next, change)

def reference(layer_input, w_qkv, w_out, w_up, w_down, gain_attn, gain_mlp, out_grad, moment_qkv, square_qkv, moment_out, square_out, moment_up, square_up, moment_down, square_down, moment_gattn, square_gattn, moment_gmlp, square_gmlp):
    weights = tuple((weight.astype(jnp.float32) for weight in (w_qkv, w_out, w_up, w_down, gain_attn, gain_mlp)))
    row_values = layer_input.astype(jnp.float32)

    def forward(weight_set, inputs):
        return lax.map(lambda seq_rows: one_sequence(weight_set, seq_rows), inputs)
    output, pullback = jax.vjp(forward, weights, row_values)
    weight_grads, input_grad = pullback(out_grad.astype(jnp.float32))
    moments = (moment_qkv, moment_out, moment_up, moment_down, moment_gattn, moment_gmlp)
    squares = (square_qkv, square_out, square_up, square_down, square_gattn, square_gmlp)
    decays = (DECAY, DECAY, DECAY, DECAY, 0.0, 0.0)
    results = [adam_step(weights[slot], weight_grads[slot], moments[slot], squares[slot], decays[slot]) for slot in range(6)]
    return (output.astype(jnp.bfloat16), input_grad.astype(jnp.bfloat16), weight_grads[0], weight_grads[1], weight_grads[2], weight_grads[3], weight_grads[4], weight_grads[5], results[0][0], results[1][0], results[2][0], results[3][0], results[4][0], results[5][0], results[0][1], results[1][1], results[2][1], results[3][1], results[4][1], results[5][1], results[0][2], results[1][2], results[2][2], results[3][2], results[4][2], results[5][2])
```

```python
import functools
import jax
import jax.numpy as jnp
from jax import lax
from jax.experimental import pallas as pl
from jax.experimental.pallas import tpu as pltpu
from jax.sharding import PartitionSpec as P


F32 = jnp.float32
BF16 = jnp.bfloat16
EPS_NORM = 1e-05
HD = 64
ROT = 16
PAIR = 2 * HD
STEP = 10
BETA_ONE = 0.9
BETA_TWO = 0.95
RATE = 0.02
DECAY = 0.1
ADAM_EPS = 1e-08


def contract_last(left, right):
    return lax.dot_general(left, right, (((1,), (1,)), ((), ())), preferred_element_type=F32)


def contract_first(left, right):
    return lax.dot_general(left, right, (((0,), (0,)), ((), ())), preferred_element_type=F32)


def plain_dot(left, right):
    return lax.dot_general(left, right, (((1,), (0,)), ((), ())), preferred_element_type=F32)


def turn(pair_values, cosine, sine):
    lane = lax.broadcasted_iota(jnp.int32, (1, PAIR), 1)
    ahead = pltpu.roll(pair_values, PAIR - ROT // 2, 1)
    behind = pltpu.roll(pair_values, ROT // 2, 1)
    return pair_values * cosine + jnp.where(lane % HD < ROT // 2, -ahead, behind) * sine


def place(i, me, count):
    return ((i // count) ^ me[0]) * count + i % count


def piece_specs(pieces, block):
    count = pieces[0].shape[0] // block

    def spec(k):
        return pl.BlockSpec(
            (block, pieces[0].shape[1]), lambda i, me: (jnp.clip(i - k * count, 0, count - 1), 0)
        )

    return [spec(k) for k in range(len(pieces))]


def take_piece(refs, held, count):
    step = pl.program_id(0)
    for k, ref in enumerate(refs):

        @pl.when(step // count == k)
        def _():
            held[...] = ref[...]

    return held[...]


def normalize(rows, gain):
    centred = rows - jnp.mean(rows, axis=-1, keepdims=True)
    spread = jnp.mean(centred * centred, axis=-1, keepdims=True)
    return (centred * lax.rsqrt(spread + EPS_NORM) * gain).astype(BF16)


def project_kernel(count, me, x0, x1, x2, x3, ga_ref, w_ref, cos_ref, sin_ref, na_ref, qkv_ref, held):
    rows = take_piece((x0, x1, x2, x3), held, count).astype(F32)
    normed = normalize(rows, ga_ref[...])
    na_ref[...] = normed
    projected = plain_dot(normed, w_ref[...])
    width = w_ref.shape[1] // 3
    cosine = cos_ref[...]
    sine = sin_ref[...]
    for start in range(0, 3 * width, PAIR):
        columns = projected[:, start : start + PAIR]
        kind = start // PAIR % 3
        if kind < 2:
            columns = turn(columns, cosine, sine)
        columns = columns.astype(BF16)
        if kind == 0:
            columns = columns * jnp.asarray(HD**-0.5, BF16)
        qkv_ref[:, start : start + PAIR] = columns


def project(me, pieces, gain_attn, weight, tables, block=256):
    tokens, dim = pieces[0].shape
    count = tokens // block
    length = 4 * tokens
    width = weight.shape[1]
    whole = lambda i, me: (0, 0)
    part = lambda i, me: (place(i, me, count), 0)
    return pl.pallas_call(
        functools.partial(project_kernel, count),
        name="project",
        grid_spec=pltpu.PrefetchScalarGridSpec(
            num_scalar_prefetch=1,
            grid=(length // block,),
            in_specs=piece_specs(pieces, block)
            + [
                pl.BlockSpec((1, dim), whole),
                pl.BlockSpec((dim, width), whole),
                pl.BlockSpec((block, PAIR), part),
                pl.BlockSpec((block, PAIR), part),
            ],
            out_specs=[
                pl.BlockSpec((block, dim), part),
                pl.BlockSpec((block, width), part),
            ],
            scratch_shapes=[pltpu.VMEM((block, dim), BF16)],
        ),
        out_shape=[
            jax.ShapeDtypeStruct((length, dim), BF16),
            jax.ShapeDtypeStruct((length, width), BF16),
        ],
        cost_estimate=pl.CostEstimate(
            flops=2 * length * dim * width, bytes_accessed=6 * length * dim + 2 * length * width, transcendentals=0
        ),
    )(me, *pieces, gain_attn, weight, *tables)


def forward_kernel(block, q_ref, k_ref, v_ref, o_ref, lse_ref, v_first, v_second):
    at = pl.program_id(1)
    lane = lax.broadcasted_iota(jnp.int32, (1, PAIR), 1)
    first = lane < HD

    @pl.when(at == 0)
    def _():
        values = v_ref[...]
        one = jnp.ones_like(values)
        v_first[...] = jnp.where(first, values, one)
        v_second[...] = jnp.where(first, one, values)

    queries = q_ref[...]
    nil = jnp.zeros_like(queries)
    q_first = jnp.where(first, queries, nil)
    q_second = jnp.where(first, nil, queries)

    def one_head(q_part, v_part, start, masked, top, total):
        keys = k_ref[pl.ds(start, block), :]
        scores = contract_last(q_part, keys)
        if masked:
            row = lax.broadcasted_iota(jnp.int32, scores.shape, 0)
            col = lax.broadcasted_iota(jnp.int32, scores.shape, 1)
            scores = jnp.where(col <= row, scores, -1e30)
        new_top = jnp.maximum(top, jnp.max(scores, axis=-1, keepdims=True))
        weights = jnp.exp(scores - new_top).astype(BF16)
        total = total * jnp.exp(top - new_top) + plain_dot(weights, v_part[pl.ds(start, block), :])
        return new_top, total

    def both(j, state, masked):
        start = pl.multiple_of(j * block, block)
        top_a, sum_a, top_b, sum_b = state
        top_a, sum_a = one_head(q_first, v_first, start, masked, top_a, sum_a)
        top_b, sum_b = one_head(q_second, v_second, start, masked, top_b, sum_b)
        return top_a, sum_a, top_b, sum_b

    low = jnp.full((block, 1), -1e30, F32)
    zero = jnp.zeros((block, PAIR), F32)
    state = both(at, (low, zero, low, zero), True)
    state = lax.fori_loop(0, at, lambda j, s: both(j, s, False), state)
    top_a, sum_a, top_b, sum_b = state
    mixed = jnp.where(first, sum_a, sum_b)
    total = jnp.where(first, pltpu.roll(sum_a, HD, 1), pltpu.roll(sum_b, HD, 1))
    o_ref[...] = (mixed / total).astype(BF16)
    lse_ref[...] = jnp.where(first, top_a, top_b) + jnp.log(total)


def attend(qkv, block=512):
    length, width3 = qkv.shape
    width = width3 // 3
    pairs = width // PAIR
    steps = length // block
    return pl.pallas_call(
        functools.partial(forward_kernel, block),
        name="attend",
        grid=(pairs, steps),
        in_specs=[
            pl.BlockSpec((block, PAIR), lambda h, i: (i, 3 * h)),
            pl.BlockSpec((length, PAIR), lambda h, i: (0, 3 * h + 1)),
            pl.BlockSpec((length, PAIR), lambda h, i: (0, 3 * h + 2)),
        ],
        out_specs=[
            pl.BlockSpec((block, PAIR), lambda h, i: (i, h)),
            pl.BlockSpec((block, PAIR), lambda h, i: (i, h)),
        ],
        out_shape=[
            jax.ShapeDtypeStruct((length, width), BF16),
            jax.ShapeDtypeStruct((length, width), F32),
        ],
        scratch_shapes=[pltpu.VMEM((length, PAIR), BF16), pltpu.VMEM((length, PAIR), BF16)],
        cost_estimate=pl.CostEstimate(
            flops=8 * length * length * width, bytes_accessed=12 * length * width, transcendentals=length * length * width // HD
        ),
    )(qkv, qkv, qkv)


def backward_kernel(
    block, q_ref, k_ref, v_ref, o_ref, do_ref, lse_ref, cos_ref, sin_ref,
    grad_ref, q_a, q_b, k_a, k_b, do_a, do_b, top_row, dot_row, dq_sum,
):
    length = q_ref.shape[0]
    steps = length // block
    lane = lax.broadcasted_iota(jnp.int32, (1, PAIR), 1)
    first = lane < HD
    ones = jnp.ones((8, PAIR), BF16)
    for i in range(steps):
        at = pl.ds(i * block, block)
        nil = jnp.zeros((block, PAIR), BF16)
        for source, left, right in ((q_ref, q_a, q_b), (k_ref, k_a, k_b), (do_ref, do_a, do_b)):
            values = source[at, :]
            left[at, :] = jnp.where(first, values, nil)
            right[at, :] = jnp.where(first, nil, values)
        product = do_ref[at, :].astype(F32) * o_ref[at, :].astype(F32)
        high_part = product.astype(BF16)
        low_part = (product - high_part.astype(F32)).astype(BF16)
        for slot, keep in ((0, first), (1, jnp.logical_not(first))):
            dot_row[8 * slot : 8 * slot + 8, at] = contract_last(
                ones, jnp.where(keep, high_part, nil)
            ) + contract_last(ones, jnp.where(keep, low_part, nil))
        turned = jnp.transpose(lse_ref[at, :])
        top_row[0:8, at] = turned[0:8, :]
        top_row[8:16, at] = turned[HD : HD + 8, :]
    dq_sum[...] = jnp.zeros_like(dq_sum)

    def one_block(i, j, key_sum, value_sum, masked):
        q_at = pl.ds(pl.multiple_of(i * block, block), block)
        k_at = pl.ds(pl.multiple_of(j * block, block), block)
        keys = k_ref[k_at, :]
        values = v_ref[k_at, :]
        for slot, q_s, k_s, do_s in ((0, q_a, k_a, do_a), (1, q_b, k_b, do_b)):
            q_part = q_s[q_at, :]
            do_part = do_s[q_at, :]
            scores = contract_last(keys, q_part)
            if masked:
                key_at = lax.broadcasted_iota(jnp.int32, scores.shape, 0)
                query_at = lax.broadcasted_iota(jnp.int32, scores.shape, 1)
                scores = jnp.where(key_at <= query_at, scores, -1e30)
            soft = jnp.exp(scores - top_row[8 * slot : 8 * slot + 1, q_at])
            value_sum = value_sum + plain_dot(soft.astype(BF16), do_part)
            grad = contract_last(values, do_part)
            grad_scores = (soft * (grad - dot_row[8 * slot : 8 * slot + 1, q_at])).astype(BF16)
            key_sum = key_sum + plain_dot(grad_scores, q_part)
            dq_sum[q_at, :] += contract_first(grad_scores, k_s[k_at, :])
        return key_sum, value_sum

    def key_block(j, carry):
        zero = jnp.zeros((block, PAIR), F32)
        state = one_block(j, j, zero, zero, True)
        state = lax.fori_loop(j + 1, steps, lambda i, s: one_block(i, j, s[0], s[1], False), state)
        k_at = pl.ds(pl.multiple_of(j * block, block), block)
        grad_ref[k_at, PAIR : 2 * PAIR] = turn(state[0], cos_ref[k_at, :], -sin_ref[k_at, :]).astype(BF16)
        grad_ref[k_at, 2 * PAIR :] = state[1].astype(BF16)
        return carry

    lax.fori_loop(0, steps, key_block, 0)
    for i in range(steps):
        at = pl.ds(i * block, block)
        turned = turn(dq_sum[at, :] * HD**-0.5, cos_ref[at, :], -sin_ref[at, :])
        grad_ref[at, :PAIR] = turned.astype(BF16)


def attend_back(qkv, context, grad_context, lse, tables, pair, block=512):
    length = qkv.shape[0]
    col = lambda at: pl.BlockSpec((length, PAIR), lambda h: (0, at))
    whole = pl.BlockSpec((length, PAIR), lambda h: (0, 0))
    return pl.pallas_call(
        functools.partial(backward_kernel, block),
        name="attend_back",
        grid=(1,),
        in_specs=[col(3 * pair), col(3 * pair + 1), col(3 * pair + 2), col(pair), col(pair), col(pair), whole, whole],
        out_specs=pl.BlockSpec((length, 3 * PAIR), lambda h: (0, 0)),
        out_shape=jax.ShapeDtypeStruct((length, 3 * PAIR), BF16),
        scratch_shapes=[pltpu.VMEM((length, PAIR), BF16)] * 6
        + [pltpu.VMEM((16, length), F32)] * 2
        + [pltpu.VMEM((length, PAIR), F32)],
        cost_estimate=pl.CostEstimate(
            flops=20 * length * length * PAIR, bytes_accessed=20 * length * PAIR, transcendentals=2 * length * length
        ),
    )(qkv, qkv, qkv, context, grad_context, lse, *tables)


def mlp_kernel(
    count, me, x0, x1, x2, x3, g0, g1, g2, g3, gain_ref, down_ref, up_ref,
    n_ref, act_ref, gh_ref, g_ref, part_ref, below_ref, x_held, g_held, up_held,
):
    fold, four_rows, hid = up_ref.shape
    rows = four_rows // 4

    @pl.when(pl.program_id(0) == 0)
    def _():
        for f in range(fold):
            for k in range(4):
                at = (k * fold + f) * rows
                up_held[at : at + rows, :] = up_ref[f, k * rows : (k + 1) * rows, :]

    gain = gain_ref[...]
    normed = normalize(take_piece((x0, x1, x2, x3), x_held, count).astype(F32), gain)
    n_ref[...] = normed
    upstream = take_piece((g0, g1, g2, g3), g_held, count)
    g_ref[...] = upstream
    down = down_ref[...].reshape(hid, down_ref.shape[2])
    up = up_held[...]
    hidden = plain_dot(normed, up)
    back = contract_last(upstream, down)
    below = 0.5 + 0.5 * lax.erf(hidden * (0.5**0.5))
    activated = (hidden * below).astype(BF16)
    slope = below + hidden * jnp.exp(-0.5 * hidden * hidden) * 0.3989422804014327
    grad_hidden = (back * slope).astype(BF16)
    act_ref[...] = activated
    gh_ref[...] = grad_hidden
    part_ref[...] = plain_dot(activated, down).astype(BF16)
    below_ref[...] = (contract_last(grad_hidden, up) * gain).astype(BF16)


def mlp(me, pieces, grad_pieces, gain_mlp, gathered, block=256):
    tokens, dim = pieces[0].shape
    length = 4 * tokens
    fold, _, hid = gathered.shape
    deep = hid // fold
    count = tokens // block
    whole = lambda i, me: (0, 0)
    part = lambda i, me: (place(i, me, count), 0)
    tile = lambda columns: pl.BlockSpec((block, columns), part)
    shape = lambda columns: jax.ShapeDtypeStruct((length, columns), BF16)
    return pl.pallas_call(
        functools.partial(mlp_kernel, count),
        name="mlp",
        grid_spec=pltpu.PrefetchScalarGridSpec(
            num_scalar_prefetch=1,
            grid=(length // block,),
            in_specs=piece_specs(pieces, block)
            + piece_specs(grad_pieces, block)
            + [
                pl.BlockSpec((1, dim), whole),
                pl.BlockSpec((fold, deep, dim), lambda i, me: (0, 0, 0)),
                pl.BlockSpec((fold, deep, hid), lambda i, me: (0, 1, 0)),
            ],
            out_specs=[tile(dim), tile(hid), tile(hid), tile(dim), tile(dim), tile(dim)],
            scratch_shapes=[
                pltpu.VMEM((block, dim), BF16),
                pltpu.VMEM((block, dim), BF16),
                pltpu.VMEM((dim, hid), BF16),
            ],
        ),
        out_shape=[shape(dim), shape(hid), shape(hid), shape(dim), shape(dim), shape(dim)],
        cost_estimate=pl.CostEstimate(
            flops=8 * length * dim * hid, bytes_accessed=16 * length * dim + 4 * dim * hid, transcendentals=2 * length * hid
        ),
    )(me, *pieces, *grad_pieces, gain_mlp, gathered, gathered)


def swap(values, axis, bit):
    ways = lax.axis_size(axis)
    return lax.ppermute(values, axis, [(i, i ^ bit) for i in range(ways)])


def bits_of(ways):
    return [1 << k for k in range(ways.bit_length() - 1)]


def bit_set(axis, bit):
    return (lax.axis_index(axis) & bit) != 0


def pick(values, at, axis):
    return lax.dynamic_index_in_dim(values, at, axis, keepdims=False)


def gather_far_first(shard, axis, at):
    held = shard
    for bit in reversed(bits_of(lax.axis_size(axis))):
        other = swap(held, axis, bit)
        upper = bit_set(axis, bit)
        held = jnp.stack([jnp.where(upper, other, held), jnp.where(upper, held, other)], axis=at)
        at += 1
    return held


def reduce_near_first(values, axis, at):
    bits = bits_of(lax.axis_size(axis))
    held = values.reshape(values.shape[:at] + (2,) * len(bits) + values.shape[at + 1 :])
    for bit in bits:
        mine = (lax.axis_index(axis) & bit) // bit
        spot = at + len(bits) - bits.index(bit) - 1
        arrived = swap(pick(held, 1 - mine, spot), axis, bit)
        held = (pick(held, mine, spot).astype(F32) + arrived.astype(F32)).astype(BF16)
    return held


def exchange(values, axis):
    ways = lax.axis_size(axis)
    me = lax.axis_index(axis)
    pieces = [pick(values, me, 0)]
    for k in range(1, ways):
        pieces.append(swap(pick(values, me ^ k, 0), axis, k))
    count = len(bits_of(ways))
    held = jnp.stack(pieces).reshape((2,) * count + pieces[0].shape)
    for spot, bit in enumerate(reversed(bits_of(ways))):
        held = jnp.where(bit_set(axis, bit), jnp.flip(held, spot), held)
    return held.reshape((ways,) + pieces[0].shape)


def gather_sequence(rows):
    near = swap(rows, "seq", 1)
    far = swap(rows, "seq", 2)
    return rows, near, far, swap(far, "seq", 1)


def sum_sequence(partial):
    me = lax.axis_index("seq")
    tokens = partial.shape[0] // 4
    held = partial.reshape(2, 2, tokens, partial.shape[1])
    mine = me & 1
    arrived = swap(pick(held, 1 - mine, 1), "seq", 1)
    held = (pick(held, mine, 1).astype(F32) + arrived.astype(F32)).astype(BF16)
    mine = me >> 1
    arrived = swap(pick(held, 1 - mine, 0), "seq", 2)
    return pick(held, mine, 0).astype(F32) + arrived.astype(F32)


def rotary_tables(length):
    lane = jnp.arange(PAIR, dtype=jnp.int32) % HD
    step = (lane % (ROT // 2)).astype(F32)
    frequency = jnp.where(lane < ROT, 10000.0 ** (-(step * 2.0) / ROT), 0.0)
    angles = jnp.arange(length, dtype=jnp.int32).astype(F32)[:, None] * frequency[None, :]
    return jnp.cos(angles), jnp.sin(angles)


def adam_step(weight, gradient, moment, square, decay_rate):
    moment_next = BETA_ONE * moment + (1.0 - BETA_ONE) * gradient
    square_next = BETA_TWO * square + (1.0 - BETA_TWO) * gradient * gradient
    moment_hat = moment_next / (1.0 - BETA_ONE**STEP)
    square_hat = square_next / (1.0 - BETA_TWO**STEP)
    change = -RATE * (
        moment_hat / (jnp.sqrt(square_hat) + ADAM_EPS) + decay_rate * weight.astype(F32)
    )
    return (moment_next, square_next, change)


def one_step(
    layer_input, w_qkv, w_out, w_up, w_down, gain_attn, gain_mlp, out_grad,
    moment_qkv, square_qkv, moment_out, square_out, moment_up, square_up, moment_down, square_down,
    moment_gattn, square_gattn, moment_gmlp, square_gmlp,
):
    ways = lax.axis_size("seq")
    fold = lax.axis_size("fsdp")
    rows = w_qkv.shape[0]
    dim = rows * ways * fold
    inner = w_qkv.shape[1] // 3
    group = inner // ways
    hid = w_up.shape[1] // ways
    tokens = layer_input.shape[1]
    length = tokens * ways

    me = lax.axis_index("seq").astype(jnp.int32).reshape(1)
    gains = gather_far_first(
        gather_far_first(jnp.stack([gain_attn, gain_mlp]), "fsdp", 1), "seq", 1
    ).reshape(2, dim).astype(F32)
    down_rows = w_down.shape[0]
    split_up = w_up.reshape(rows, ways, hid).transpose(1, 0, 2)
    local_up = exchange(split_up, "seq").reshape(ways * rows, hid)
    later = lax.all_gather(jnp.concatenate([w_down, local_up]), "fsdp")
    local_rows = layer_input[0]
    row_pieces = gather_sequence(local_rows)
    grad_pieces = gather_sequence(out_grad[0])
    count = group // PAIR
    split_qkv = (
        w_qkv.reshape(rows, 3, ways, count, PAIR).transpose(2, 0, 3, 1, 4).reshape(ways, rows, 3 * group)
    )
    local_qkv = exchange(split_qkv, "seq")
    full_qkv = gather_far_first(local_qkv, "fsdp", 1).reshape(dim, 3 * group)
    full_out = gather_far_first(w_out, "fsdp", 0).reshape(fold * rows, dim)
    tables = rotary_tables(length)

    normed_mlp, activated, grad_hidden, upstream, partial, mlp_term = mlp(
        me, row_pieces, grad_pieces, gains[1:2], later
    )
    grad_wdown = contract_first(activated, upstream).astype(BF16)
    grad_wup = contract_first(normed_mlp, grad_hidden).astype(BF16)
    sendable = jnp.concatenate(
        [
            grad_wdown.reshape(fold, down_rows, dim),
            grad_wup.reshape(ways, fold, rows, hid).transpose(1, 0, 2, 3).reshape(fold, ways * rows, hid),
        ],
        axis=1,
    )
    pair_weights = [full_qkv[:, 3 * PAIR * pair : 3 * PAIR * (pair + 1)] for pair in range(count)]
    sendable, full_qkv, pair_weights = lax.optimization_barrier((sendable, full_qkv, pair_weights))
    owned_sum = lax.psum_scatter(sendable, "fsdp", scatter_dimension=0)
    sum_down = owned_sum[:down_rows].astype(F32)
    back_up = exchange(owned_sum[down_rows:].reshape(ways, rows, hid), "seq")
    sum_up = back_up.transpose(1, 0, 2).reshape(rows, ways * hid).astype(F32)

    normed_attn, qkv = project(me, row_pieces, gains[0:1], full_qkv, tables)
    context, lse = attend(qkv)
    grad_context = contract_last(upstream, full_out).astype(BF16)
    partial = (plain_dot(context, full_out) + partial.astype(F32)).astype(BF16)
    grad_wout = contract_first(context, upstream).astype(BF16)
    grad_context, partial, grad_wout = lax.optimization_barrier((grad_context, partial, grad_wout))
    branch = sum_sequence(partial)
    layer_output = (local_rows.astype(F32) + branch).astype(BF16)[None]
    sum_out = reduce_near_first(grad_wout.reshape(fold, rows, dim), "fsdp", 0).astype(F32)

    upper = mlp_term.astype(F32)
    near_pairs = []
    for pair in range(count):
        grad_pair = attend_back(qkv, context, grad_context, lse, tables, pair)
        grad_weight = contract_first(normed_attn, grad_pair).astype(BF16)
        if pair + 1 < count:
            grad_weight, grad_context = lax.optimization_barrier((grad_weight, grad_context))
        near = reduce_near_first(grad_weight.reshape(ways, fold, rows, 3 * PAIR), "fsdp", 1)
        near_pairs.append(near)
        upper = upper + contract_last(grad_pair, pair_weights[pair]) * gains[0:1]
    near_qkv = jnp.concatenate(near_pairs, axis=2)
    back_qkv = exchange(near_qkv, "seq")
    sum_qkv = (
        back_qkv.reshape(ways, rows, count, 3, PAIR).transpose(1, 3, 0, 2, 4).reshape(rows, 3 * inner).astype(F32)
    )

    upper = sum_sequence(upper.astype(BF16))
    local = local_rows.astype(F32)
    centred = local - jnp.mean(local, axis=-1, keepdims=True)
    inverse = lax.rsqrt(jnp.mean(centred * centred, axis=-1, keepdims=True) + EPS_NORM)
    xhat = centred * inverse
    term = inverse * (
        upper
        - jnp.mean(upper, axis=-1, keepdims=True)
        - xhat * jnp.mean(upper * xhat, axis=-1, keepdims=True)
    )
    input_grad = (out_grad[0].astype(F32) + term).astype(BF16)[None]

    sum_gattn = jnp.sum(w_qkv.astype(F32) * sum_qkv, axis=1) / gain_attn.astype(F32)
    sum_gmlp = jnp.sum(w_up.astype(F32) * sum_up, axis=1) / gain_mlp.astype(F32)
    summed = (sum_qkv, sum_out, sum_up, sum_down, sum_gattn, sum_gmlp)
    owned = (w_qkv, w_out, w_up, w_down, gain_attn, gain_mlp)
    moments = (moment_qkv, moment_out, moment_up, moment_down, moment_gattn, moment_gmlp)
    squares = (square_qkv, square_out, square_up, square_down, square_gattn, square_gmlp)
    decays = (DECAY, DECAY, DECAY, DECAY, 0.0, 0.0)
    results = [
        adam_step(owned[slot], summed[slot], moments[slot], squares[slot], decays[slot])
        for slot in range(6)
    ]
    return (
        (layer_output, input_grad)
        + summed
        + tuple(result[0] for result in results)
        + tuple(result[1] for result in results)
        + tuple(result[2] for result in results)
    )


def solution(mesh):
    acts = P("fsdp", "seq", None)
    mat = P(("seq", "fsdp"), None)
    vec = P(("seq", "fsdp"))
    six = (mat, mat, mat, mat, vec, vec)
    return jax.shard_map(
        one_step,
        mesh=mesh,
        in_specs=(acts,) + six + (acts,) + (mat,) * 8 + (vec,) * 4,
        out_specs=(acts, acts) + six * 4,
        check_vma=False,
    )
```

```python
import functools
import jax
import jax.numpy as jnp
from jax import lax
from jax.experimental import pallas as pl
from jax.experimental.pallas import tpu as pltpu
from jax.sharding import PartitionSpec as P


F32 = jnp.float32
BF16 = jnp.bfloat16
EPS_NORM = 1e-05
HD = 64
ROT = 16
PAIR = 2 * HD
STEP = 10
BETA_ONE = 0.9
BETA_TWO = 0.95
RATE = 0.02
DECAY = 0.1
ADAM_EPS = 1e-08


def contract_last(left, right):
    return lax.dot_general(left, right, (((1,), (1,)), ((), ())), preferred_element_type=F32)


def contract_first(left, right):
    return lax.dot_general(left, right, (((0,), (0,)), ((), ())), preferred_element_type=F32)


def plain_dot(left, right):
    return lax.dot_general(left, right, (((1,), (0,)), ((), ())), preferred_element_type=F32)


def turn(pair_values, cosine, sine):
    lane = lax.broadcasted_iota(jnp.int32, (1, PAIR), 1)
    ahead = pltpu.roll(pair_values, PAIR - ROT // 2, 1)
    behind = pltpu.roll(pair_values, ROT // 2, 1)
    return pair_values * cosine + jnp.where(lane % HD < ROT // 2, -ahead, behind) * sine


def place(i, me, count):
    return ((i // count) ^ me[0]) * count + i % count


def piece_specs(pieces, block):
    count = pieces[0].shape[0] // block

    def spec(k):
        return pl.BlockSpec(
            (block, pieces[0].shape[1]), lambda i, me: (jnp.clip(i - k * count, 0, count - 1), 0)
        )

    return [spec(k) for k in range(len(pieces))]


def take_piece(refs, held, count):
    step = pl.program_id(0)
    for k, ref in enumerate(refs):

        @pl.when(step // count == k)
        def _():
            held[...] = ref[...]

    return held[...]


def normalize(rows, gain):
    centred = rows - jnp.mean(rows, axis=-1, keepdims=True)
    spread = jnp.mean(centred * centred, axis=-1, keepdims=True)
    return (centred * lax.rsqrt(spread + EPS_NORM) * gain).astype(BF16)


def project_kernel(count, me, x0, x1, x2, x3, ga_ref, w_ref, cos_ref, sin_ref, na_ref, qkv_ref, held):
    rows = take_piece((x0, x1, x2, x3), held, count).astype(F32)
    normed = normalize(rows, ga_ref[...])
    na_ref[...] = normed
    projected = plain_dot(normed, w_ref[...])
    width = w_ref.shape[1] // 3
    cosine = cos_ref[...]
    sine = sin_ref[...]
    for start in range(0, 3 * width, PAIR):
        columns = projected[:, start : start + PAIR]
        kind = start // PAIR % 3
        if kind < 2:
            columns = turn(columns, cosine, sine)
        columns = columns.astype(BF16)
        if kind == 0:
            columns = columns * jnp.asarray(HD**-0.5, BF16)
        qkv_ref[:, start : start + PAIR] = columns


def project(me, pieces, gain_attn, weight, tables, block=256):
    tokens, dim = pieces[0].shape
    count = tokens // block
    length = 4 * tokens
    width = weight.shape[1]
    whole = lambda i, me: (0, 0)
    part = lambda i, me: (place(i, me, count), 0)
    return pl.pallas_call(
        functools.partial(project_kernel, count),
        name="project",
        grid_spec=pltpu.PrefetchScalarGridSpec(
            num_scalar_prefetch=1,
            grid=(length // block,),
            in_specs=piece_specs(pieces, block)
            + [
                pl.BlockSpec((1, dim), whole),
                pl.BlockSpec((dim, width), whole),
                pl.BlockSpec((block, PAIR), part),
                pl.BlockSpec((block, PAIR), part),
            ],
            out_specs=[
                pl.BlockSpec((block, dim), part),
                pl.BlockSpec((block, width), part),
            ],
            scratch_shapes=[pltpu.VMEM((block, dim), BF16)],
        ),
        out_shape=[
            jax.ShapeDtypeStruct((length, dim), BF16),
            jax.ShapeDtypeStruct((length, width), BF16),
        ],
        cost_estimate=pl.CostEstimate(
            flops=2 * length * dim * width, bytes_accessed=6 * length * dim + 2 * length * width, transcendentals=0
        ),
    )(me, *pieces, gain_attn, weight, *tables)


def forward_kernel(block, q_ref, k_ref, v_ref, o_ref, lse_ref, v_first, v_second):
    at = pl.program_id(1)
    lane = lax.broadcasted_iota(jnp.int32, (1, PAIR), 1)
    first = lane < HD

    @pl.when(at == 0)
    def _():
        values = v_ref[...]
        one = jnp.ones_like(values)
        v_first[...] = jnp.where(first, values, one)
        v_second[...] = jnp.where(first, one, values)

    queries = q_ref[...]
    nil = jnp.zeros_like(queries)
    q_first = jnp.where(first, queries, nil)
    q_second = jnp.where(first, nil, queries)

    def one_head(q_part, v_part, start, masked, top, total):
        keys = k_ref[pl.ds(start, block), :]
        scores = contract_last(q_part, keys)
        if masked:
            row = lax.broadcasted_iota(jnp.int32, scores.shape, 0)
            col = lax.broadcasted_iota(jnp.int32, scores.shape, 1)
            scores = jnp.where(col <= row, scores, -1e30)
        new_top = jnp.maximum(top, jnp.max(scores, axis=-1, keepdims=True))
        weights = jnp.exp(scores - new_top).astype(BF16)
        total = total * jnp.exp(top - new_top) + plain_dot(weights, v_part[pl.ds(start, block), :])
        return new_top, total

    def both(j, state, masked):
        start = pl.multiple_of(j * block, block)
        top_a, sum_a, top_b, sum_b = state
        top_a, sum_a = one_head(q_first, v_first, start, masked, top_a, sum_a)
        top_b, sum_b = one_head(q_second, v_second, start, masked, top_b, sum_b)
        return top_a, sum_a, top_b, sum_b

    low = jnp.full((block, 1), -1e30, F32)
    zero = jnp.zeros((block, PAIR), F32)
    state = both(at, (low, zero, low, zero), True)
    state = lax.fori_loop(0, at, lambda j, s: both(j, s, False), state)
    top_a, sum_a, top_b, sum_b = state
    mixed = jnp.where(first, sum_a, sum_b)
    total = jnp.where(first, pltpu.roll(sum_a, HD, 1), pltpu.roll(sum_b, HD, 1))
    o_ref[...] = (mixed / total).astype(BF16)
    lse_ref[...] = jnp.where(first, top_a, top_b) + jnp.log(total)


def attend(qkv, block=512):
    length, width3 = qkv.shape
    width = width3 // 3
    pairs = width // PAIR
    steps = length // block
    return pl.pallas_call(
        functools.partial(forward_kernel, block),
        name="attend",
        grid=(pairs, steps),
        in_specs=[
            pl.BlockSpec((block, PAIR), lambda h, i: (i, 3 * h)),
            pl.BlockSpec((length, PAIR), lambda h, i: (0, 3 * h + 1)),
            pl.BlockSpec((length, PAIR), lambda h, i: (0, 3 * h + 2)),
        ],
        out_specs=[
            pl.BlockSpec((block, PAIR), lambda h, i: (i, h)),
            pl.BlockSpec((block, PAIR), lambda h, i: (i, h)),
        ],
        out_shape=[
            jax.ShapeDtypeStruct((length, width), BF16),
            jax.ShapeDtypeStruct((length, width), F32),
        ],
        scratch_shapes=[pltpu.VMEM((length, PAIR), BF16), pltpu.VMEM((length, PAIR), BF16)],
        cost_estimate=pl.CostEstimate(
            flops=8 * length * length * width, bytes_accessed=12 * length * width, transcendentals=length * length * width // HD
        ),
    )(qkv, qkv, qkv)


def backward_kernel(
    block, q_ref, k_ref, v_ref, o_ref, do_ref, lse_ref, cos_ref, sin_ref,
    grad_ref, q_a, q_b, k_a, k_b, do_a, do_b, top_row, dot_row, dq_sum,
):
    length = q_ref.shape[0]
    steps = length // block
    lane = lax.broadcasted_iota(jnp.int32, (1, PAIR), 1)
    first = lane < HD
    ones = jnp.ones((8, PAIR), BF16)
    for i in range(steps):
        at = pl.ds(i * block, block)
        nil = jnp.zeros((block, PAIR), BF16)
        for source, left, right in ((q_ref, q_a, q_b), (k_ref, k_a, k_b), (do_ref, do_a, do_b)):
            values = source[at, :]
            left[at, :] = jnp.where(first, values, nil)
            right[at, :] = jnp.where(first, nil, values)
        product = do_ref[at, :].astype(F32) * o_ref[at, :].astype(F32)
        high_part = product.astype(BF16)
        low_part = (product - high_part.astype(F32)).astype(BF16)
        for slot, keep in ((0, first), (1, jnp.logical_not(first))):
            dot_row[8 * slot : 8 * slot + 8, at] = contract_last(
                ones, jnp.where(keep, high_part, nil)
            ) + contract_last(ones, jnp.where(keep, low_part, nil))
        turned = jnp.transpose(lse_ref[at, :])
        top_row[0:8, at] = turned[0:8, :]
        top_row[8:16, at] = turned[HD : HD + 8, :]
    dq_sum[...] = jnp.zeros_like(dq_sum)

    def one_block(i, j, key_sum, value_sum, masked):
        q_at = pl.ds(pl.multiple_of(i * block, block), block)
        k_at = pl.ds(pl.multiple_of(j * block, block), block)
        keys = k_ref[k_at, :]
        values = v_ref[k_at, :]
        for slot, q_s, k_s, do_s in ((0, q_a, k_a, do_a), (1, q_b, k_b, do_b)):
            q_part = q_s[q_at, :]
            do_part = do_s[q_at, :]
            scores = contract_last(keys, q_part)
            if masked:
                key_at = lax.broadcasted_iota(jnp.int32, scores.shape, 0)
                query_at = lax.broadcasted_iota(jnp.int32, scores.shape, 1)
                scores = jnp.where(key_at <= query_at, scores, -1e30)
            soft = jnp.exp(scores - top_row[8 * slot : 8 * slot + 1, q_at])
            value_sum = value_sum + plain_dot(soft.astype(BF16), do_part)
            grad = contract_last(values, do_part)
            grad_scores = (soft * (grad - dot_row[8 * slot : 8 * slot + 1, q_at])).astype(BF16)
            key_sum = key_sum + plain_dot(grad_scores, q_part)
            dq_sum[q_at, :] += contract_first(grad_scores, k_s[k_at, :])
        return key_sum, value_sum

    def key_block(j, carry):
        zero = jnp.zeros((block, PAIR), F32)
        state = one_block(j, j, zero, zero, True)
        state = lax.fori_loop(j + 1, steps, lambda i, s: one_block(i, j, s[0], s[1], False), state)
        k_at = pl.ds(pl.multiple_of(j * block, block), block)
        grad_ref[k_at, PAIR : 2 * PAIR] = turn(state[0], cos_ref[k_at, :], -sin_ref[k_at, :]).astype(BF16)
        grad_ref[k_at, 2 * PAIR :] = state[1].astype(BF16)
        return carry

    lax.fori_loop(0, steps, key_block, 0)
    for i in range(steps):
        at = pl.ds(i * block, block)
        turned = turn(dq_sum[at, :] * HD**-0.5, cos_ref[at, :], -sin_ref[at, :])
        grad_ref[at, :PAIR] = turned.astype(BF16)


def attend_back(qkv, context, grad_context, lse, tables, pair, block=512):
    length = qkv.shape[0]
    col = lambda at: pl.BlockSpec((length, PAIR), lambda h: (0, at))
    whole = pl.BlockSpec((length, PAIR), lambda h: (0, 0))
    return pl.pallas_call(
        functools.partial(backward_kernel, block),
        name="attend_back",
        grid=(1,),
        in_specs=[col(3 * pair), col(3 * pair + 1), col(3 * pair + 2), col(pair), col(pair), col(pair), whole, whole],
        out_specs=pl.BlockSpec((length, 3 * PAIR), lambda h: (0, 0)),
        out_shape=jax.ShapeDtypeStruct((length, 3 * PAIR), BF16),
        scratch_shapes=[pltpu.VMEM((length, PAIR), BF16)] * 6
        + [pltpu.VMEM((16, length), F32)] * 2
        + [pltpu.VMEM((length, PAIR), F32)],
        cost_estimate=pl.CostEstimate(
            flops=20 * length * length * PAIR, bytes_accessed=20 * length * PAIR, transcendentals=2 * length * length
        ),
    )(qkv, qkv, qkv, context, grad_context, lse, *tables)


def mlp_kernel(
    count, me, x0, x1, x2, x3, g0, g1, g2, g3, gain_ref, down_ref, up_ref,
    n_ref, act_ref, gh_ref, g_ref, part_ref, below_ref, x_held, g_held, up_held,
):
    fold, four_rows, hid = up_ref.shape
    rows = four_rows // 4

    @pl.when(pl.program_id(0) == 0)
    def _():
        for f in range(fold):
            for k in range(4):
                at = (k * fold + f) * rows
                up_held[at : at + rows, :] = up_ref[f, k * rows : (k + 1) * rows, :]

    gain = gain_ref[...]
    normed = normalize(take_piece((x0, x1, x2, x3), x_held, count).astype(F32), gain)
    n_ref[...] = normed
    upstream = take_piece((g0, g1, g2, g3), g_held, count)
    g_ref[...] = upstream
    down = down_ref[...].reshape(hid, down_ref.shape[2])
    up = up_held[...]
    hidden = plain_dot(normed, up)
    back = contract_last(upstream, down)
    below = 0.5 + 0.5 * lax.erf(hidden * (0.5**0.5))
    activated = (hidden * below).astype(BF16)
    slope = below + hidden * jnp.exp(-0.5 * hidden * hidden) * 0.3989422804014327
    grad_hidden = (back * slope).astype(BF16)
    act_ref[...] = activated
    gh_ref[...] = grad_hidden
    part_ref[...] = plain_dot(activated, down).astype(BF16)
    below_ref[...] = (contract_last(grad_hidden, up) * gain).astype(BF16)


def mlp(me, pieces, grad_pieces, gain_mlp, gathered, block=256):
    tokens, dim = pieces[0].shape
    length = 4 * tokens
    fold, _, hid = gathered.shape
    deep = hid // fold
    count = tokens // block
    whole = lambda i, me: (0, 0)
    part = lambda i, me: (place(i, me, count), 0)
    tile = lambda columns: pl.BlockSpec((block, columns), part)
    shape = lambda columns: jax.ShapeDtypeStruct((length, columns), BF16)
    return pl.pallas_call(
        functools.partial(mlp_kernel, count),
        name="mlp",
        grid_spec=pltpu.PrefetchScalarGridSpec(
            num_scalar_prefetch=1,
            grid=(length // block,),
            in_specs=piece_specs(pieces, block)
            + piece_specs(grad_pieces, block)
            + [
                pl.BlockSpec((1, dim), whole),
                pl.BlockSpec((fold, deep, dim), lambda i, me: (0, 0, 0)),
                pl.BlockSpec((fold, deep, hid), lambda i, me: (0, 1, 0)),
            ],
            out_specs=[tile(dim), tile(hid), tile(hid), tile(dim), tile(dim), tile(dim)],
            scratch_shapes=[
                pltpu.VMEM((block, dim), BF16),
                pltpu.VMEM((block, dim), BF16),
                pltpu.VMEM((dim, hid), BF16),
            ],
        ),
        out_shape=[shape(dim), shape(hid), shape(hid), shape(dim), shape(dim), shape(dim)],
        cost_estimate=pl.CostEstimate(
            flops=8 * length * dim * hid, bytes_accessed=16 * length * dim + 4 * dim * hid, transcendentals=2 * length * hid
        ),
    )(me, *pieces, *grad_pieces, gain_mlp, gathered, gathered)


def swap(values, axis, bit):
    ways = lax.axis_size(axis)
    return lax.ppermute(values, axis, [(i, i ^ bit) for i in range(ways)])


def bits_of(ways):
    return [1 << k for k in range(ways.bit_length() - 1)]


def bit_set(axis, bit):
    return (lax.axis_index(axis) & bit) != 0


def pick(values, at, axis):
    return lax.dynamic_index_in_dim(values, at, axis, keepdims=False)


def gather_far_first(shard, axis, at):
    held = shard
    for bit in reversed(bits_of(lax.axis_size(axis))):
        other = swap(held, axis, bit)
        upper = bit_set(axis, bit)
        held = jnp.stack([jnp.where(upper, other, held), jnp.where(upper, held, other)], axis=at)
        at += 1
    return held


def reduce_near_first(values, axis, at):
    bits = bits_of(lax.axis_size(axis))
    held = values.reshape(values.shape[:at] + (2,) * len(bits) + values.shape[at + 1 :])
    for bit in bits:
        mine = (lax.axis_index(axis) & bit) // bit
        spot = at + len(bits) - bits.index(bit) - 1
        arrived = swap(pick(held, 1 - mine, spot), axis, bit)
        held = (pick(held, mine, spot).astype(F32) + arrived.astype(F32)).astype(BF16)
    return held


def exchange(values, axis):
    ways = lax.axis_size(axis)
    me = lax.axis_index(axis)
    pieces = [pick(values, me, 0)]
    for k in range(1, ways):
        pieces.append(swap(pick(values, me ^ k, 0), axis, k))
    count = len(bits_of(ways))
    held = jnp.stack(pieces).reshape((2,) * count + pieces[0].shape)
    for spot, bit in enumerate(reversed(bits_of(ways))):
        held = jnp.where(bit_set(axis, bit), jnp.flip(held, spot), held)
    return held.reshape((ways,) + pieces[0].shape)


def gather_sequence(rows):
    near = swap(rows, "seq", 1)
    far = swap(rows, "seq", 2)
    return rows, near, far, swap(far, "seq", 1)


def sum_sequence(partial):
    me = lax.axis_index("seq")
    tokens = partial.shape[0] // 4
    held = partial.reshape(2, 2, tokens, partial.shape[1])
    mine = me & 1
    arrived = swap(pick(held, 1 - mine, 1), "seq", 1)
    held = (pick(held, mine, 1).astype(F32) + arrived.astype(F32)).astype(BF16)
    mine = me >> 1
    arrived = swap(pick(held, 1 - mine, 0), "seq", 2)
    return pick(held, mine, 0).astype(F32) + arrived.astype(F32)


def rotary_tables(length):
    lane = jnp.arange(PAIR, dtype=jnp.int32) % HD
    step = (lane % (ROT // 2)).astype(F32)
    frequency = jnp.where(lane < ROT, 10000.0 ** (-(step * 2.0) / ROT), 0.0)
    angles = jnp.arange(length, dtype=jnp.int32).astype(F32)[:, None] * frequency[None, :]
    return jnp.cos(angles), jnp.sin(angles)


def adam_step(weight, gradient, moment, square, decay_rate):
    moment_next = BETA_ONE * moment + (1.0 - BETA_ONE) * gradient
    square_next = BETA_TWO * square + (1.0 - BETA_TWO) * gradient * gradient
    moment_hat = moment_next / (1.0 - BETA_ONE**STEP)
    square_hat = square_next / (1.0 - BETA_TWO**STEP)
    change = -RATE * (
        moment_hat / (jnp.sqrt(square_hat) + ADAM_EPS) + decay_rate * weight.astype(F32)
    )
    return (moment_next, square_next, change)


def one_step(
    layer_input, w_qkv, w_out, w_up, w_down, gain_attn, gain_mlp, out_grad,
    moment_qkv, square_qkv, moment_out, square_out, moment_up, square_up, moment_down, square_down,
    moment_gattn, square_gattn, moment_gmlp, square_gmlp,
):
    ways = lax.axis_size("seq")
    fold = lax.axis_size("fsdp")
    rows = w_qkv.shape[0]
    dim = rows * ways * fold
    inner = w_qkv.shape[1] // 3
    group = inner // ways
    hid = w_up.shape[1] // ways
    tokens = layer_input.shape[1]
    length = tokens * ways

    me = lax.axis_index("seq").astype(jnp.int32).reshape(1)
    gains = gather_far_first(
        gather_far_first(jnp.stack([gain_attn, gain_mlp]), "seq", 1), "fsdp", 3
    ).reshape(2, dim).astype(F32)
    down_rows = w_down.shape[0]
    split_up = w_up.reshape(rows, ways, hid).transpose(1, 0, 2)
    local_up = exchange(split_up, "seq").reshape(ways * rows, hid)
    later = lax.all_gather(jnp.concatenate([w_down, local_up]), "fsdp")
    local_rows = layer_input[0]
    row_pieces = gather_sequence(local_rows)
    grad_pieces = gather_sequence(out_grad[0])
    count = group // PAIR
    split_qkv = (
        w_qkv.reshape(rows, 3, ways, count, PAIR).transpose(2, 0, 3, 1, 4).reshape(ways, rows, 3 * group)
    )
    local_qkv = exchange(split_qkv, "seq")
    full_qkv = gather_far_first(local_qkv, "fsdp", 1).reshape(dim, 3 * group)
    full_out = gather_far_first(w_out, "fsdp", 0).reshape(fold * rows, dim)
    tables = rotary_tables(length)

    normed_mlp, activated, grad_hidden, upstream, partial, mlp_term = mlp(
        me, row_pieces, grad_pieces, gains[1:2], later
    )
    grad_wdown = contract_first(activated, upstream).astype(BF16)
    grad_wup = contract_first(normed_mlp, grad_hidden).astype(BF16)
    sendable = jnp.concatenate(
        [
            grad_wdown.reshape(fold, down_rows, dim),
            grad_wup.reshape(ways, fold, rows, hid).transpose(1, 0, 2, 3).reshape(fold, ways * rows, hid),
        ],
        axis=1,
    )
    sendable, full_qkv = lax.optimization_barrier((sendable, full_qkv))
    owned_sum = lax.psum_scatter(sendable, "fsdp", scatter_dimension=0)

    normed_attn, qkv = project(me, row_pieces, gains[0:1], full_qkv, tables)
    context, lse = attend(qkv)
    grad_context = contract_last(upstream, full_out).astype(BF16)
    partial = (plain_dot(context, full_out) + partial.astype(F32)).astype(BF16)
    grad_wout = contract_first(context, upstream).astype(BF16)
    grad_context, partial, grad_wout = lax.optimization_barrier((grad_context, partial, grad_wout))
    branch = sum_sequence(partial)
    layer_output = (local_rows.astype(F32) + branch).astype(BF16)[None]
    sum_out = reduce_near_first(grad_wout.reshape(fold, rows, dim), "fsdp", 0).astype(F32)

    near_pairs = []
    grad_pairs = []
    for pair in range(count):
        grad_pair = attend_back(qkv, context, grad_context, lse, tables, pair)
        if pair + 1 == count:
            grad_pair, owned_sum = lax.optimization_barrier((grad_pair, owned_sum))
        grad_weight = contract_first(normed_attn, grad_pair).astype(BF16)
        if pair + 1 < count:
            grad_weight, grad_context = lax.optimization_barrier((grad_weight, grad_context))
        near = reduce_near_first(grad_weight.reshape(ways, fold, rows, 3 * PAIR), "fsdp", 1)
        near_pairs.append(near)
        grad_pairs.append(grad_pair)
    upper = (
        contract_last(jnp.concatenate(grad_pairs, axis=1), full_qkv) * gains[0:1] + mlp_term.astype(F32)
    ).astype(BF16)
    sum_down = owned_sum[:down_rows].astype(F32)
    back_up = exchange(owned_sum[down_rows:].reshape(ways, rows, hid), "seq")
    sum_up = back_up.transpose(1, 0, 2).reshape(rows, ways * hid).astype(F32)
    near_qkv = jnp.concatenate(near_pairs, axis=2)
    back_qkv = exchange(near_qkv, "seq")
    sum_qkv = (
        back_qkv.reshape(ways, rows, count, 3, PAIR).transpose(1, 3, 0, 2, 4).reshape(rows, 3 * inner).astype(F32)
    )

    upper = sum_sequence(upper)
    local = local_rows.astype(F32)
    centred = local - jnp.mean(local, axis=-1, keepdims=True)
    inverse = lax.rsqrt(jnp.mean(centred * centred, axis=-1, keepdims=True) + EPS_NORM)
    xhat = centred * inverse
    term = inverse * (
        upper
        - jnp.mean(upper, axis=-1, keepdims=True)
        - xhat * jnp.mean(upper * xhat, axis=-1, keepdims=True)
    )
    input_grad = (out_grad[0].astype(F32) + term).astype(BF16)[None]

    sum_gattn = jnp.sum(w_qkv.astype(F32) * sum_qkv, axis=1) / gain_attn.astype(F32)
    sum_gmlp = jnp.sum(w_up.astype(F32) * sum_up, axis=1) / gain_mlp.astype(F32)
    summed = (sum_qkv, sum_out, sum_up, sum_down, sum_gattn, sum_gmlp)
    owned = (w_qkv, w_out, w_up, w_down, gain_attn, gain_mlp)
    moments = (moment_qkv, moment_out, moment_up, moment_down, moment_gattn, moment_gmlp)
    squares = (square_qkv, square_out, square_up, square_down, square_gattn, square_gmlp)
    decays = (DECAY, DECAY, DECAY, DECAY, 0.0, 0.0)
    results = [
        adam_step(owned[slot], summed[slot], moments[slot], squares[slot], decays[slot])
        for slot in range(6)
    ]
    return (
        (layer_output, input_grad)
        + summed
        + tuple(result[0] for result in results)
        + tuple(result[1] for result in results)
        + tuple(result[2] for result in results)
    )


def solution(mesh):
    acts = P("fsdp", "seq", None)
    mat = P(("seq", "fsdp"), None)
    vec = P(("seq", "fsdp"))
    six = (mat, mat, mat, mat, vec, vec)
    return jax.shard_map(
        one_step,
        mesh=mesh,
        in_specs=(acts,) + six + (acts,) + (mat,) * 8 + (vec,) * 4,
        out_specs=(acts, acts) + six * 4,
        check_vma=False,
    )
```

```python
import functools
import jax
import jax.numpy as jnp
from jax import lax
from jax.experimental import pallas as pl
from jax.experimental.pallas import tpu as pltpu
from jax.sharding import PartitionSpec as P


F32 = jnp.float32
BF16 = jnp.bfloat16
EPS_NORM = 1e-05
HD = 64
ROT = 16
PAIR = 2 * HD
STEP = 10
BETA_ONE = 0.9
BETA_TWO = 0.95
RATE = 0.02
DECAY = 0.1
ADAM_EPS = 1e-08


def contract_last(left, right):
    return lax.dot_general(left, right, (((1,), (1,)), ((), ())), preferred_element_type=F32)


def contract_first(left, right):
    return lax.dot_general(left, right, (((0,), (0,)), ((), ())), preferred_element_type=F32)


def plain_dot(left, right):
    return lax.dot_general(left, right, (((1,), (0,)), ((), ())), preferred_element_type=F32)


def turn(pair_values, cosine, sine):
    lane = lax.broadcasted_iota(jnp.int32, (1, PAIR), 1)
    ahead = pltpu.roll(pair_values, PAIR - ROT // 2, 1)
    behind = pltpu.roll(pair_values, ROT // 2, 1)
    return pair_values * cosine + jnp.where(lane % HD < ROT // 2, -ahead, behind) * sine


def place(i, me, count):
    return ((i // count) ^ me[0]) * count + i % count


def piece_specs(pieces, block):
    count = pieces[0].shape[0] // block

    def spec(k):
        return pl.BlockSpec(
            (block, pieces[0].shape[1]), lambda i, me: (jnp.clip(i - k * count, 0, count - 1), 0)
        )

    return [spec(k) for k in range(len(pieces))]


def take_piece(refs, held, count):
    step = pl.program_id(0)
    for k, ref in enumerate(refs):

        @pl.when(step // count == k)
        def _():
            held[...] = ref[...]

    return held[...]


def normalize(rows, gain):
    centred = rows - jnp.mean(rows, axis=-1, keepdims=True)
    spread = jnp.mean(centred * centred, axis=-1, keepdims=True)
    return (centred * lax.rsqrt(spread + EPS_NORM) * gain).astype(BF16)


def project_kernel(count, me, x0, x1, x2, x3, ga_ref, w_ref, cos_ref, sin_ref, na_ref, qkv_ref, held):
    rows = take_piece((x0, x1, x2, x3), held, count).astype(F32)
    normed = normalize(rows, ga_ref[...])
    na_ref[...] = normed
    projected = plain_dot(normed, w_ref[...])
    width = w_ref.shape[1] // 3
    cosine = cos_ref[...]
    sine = sin_ref[...]
    for start in range(0, 3 * width, PAIR):
        columns = projected[:, start : start + PAIR]
        kind = start // PAIR % 3
        if kind < 2:
            columns = turn(columns, cosine, sine)
        columns = columns.astype(BF16)
        if kind == 0:
            columns = columns * jnp.asarray(HD**-0.5, BF16)
        qkv_ref[:, start : start + PAIR] = columns


def project(me, pieces, gain_attn, weight, tables, block=256):
    tokens, dim = pieces[0].shape
    count = tokens // block
    length = 4 * tokens
    width = weight.shape[1]
    whole = lambda i, me: (0, 0)
    part = lambda i, me: (place(i, me, count), 0)
    return pl.pallas_call(
        functools.partial(project_kernel, count),
        name="project",
        grid_spec=pltpu.PrefetchScalarGridSpec(
            num_scalar_prefetch=1,
            grid=(length // block,),
            in_specs=piece_specs(pieces, block)
            + [
                pl.BlockSpec((1, dim), whole),
                pl.BlockSpec((dim, width), whole),
                pl.BlockSpec((block, PAIR), part),
                pl.BlockSpec((block, PAIR), part),
            ],
            out_specs=[
                pl.BlockSpec((block, dim), part),
                pl.BlockSpec((block, width), part),
            ],
            scratch_shapes=[pltpu.VMEM((block, dim), BF16)],
        ),
        out_shape=[
            jax.ShapeDtypeStruct((length, dim), BF16),
            jax.ShapeDtypeStruct((length, width), BF16),
        ],
        cost_estimate=pl.CostEstimate(
            flops=2 * length * dim * width, bytes_accessed=6 * length * dim + 2 * length * width, transcendentals=0
        ),
    )(me, *pieces, gain_attn, weight, *tables)


def forward_kernel(block, q_ref, k_ref, v_ref, o_ref, lse_ref, v_first, v_second):
    at = pl.program_id(1)
    lane = lax.broadcasted_iota(jnp.int32, (1, PAIR), 1)
    first = lane < HD

    @pl.when(at == 0)
    def _():
        values = v_ref[...]
        one = jnp.ones_like(values)
        v_first[...] = jnp.where(first, values, one)
        v_second[...] = jnp.where(first, one, values)

    queries = q_ref[...]
    nil = jnp.zeros_like(queries)
    q_first = jnp.where(first, queries, nil)
    q_second = jnp.where(first, nil, queries)

    def one_head(q_part, v_part, start, masked, top, total):
        keys = k_ref[pl.ds(start, block), :]
        scores = contract_last(q_part, keys)
        if masked:
            row = lax.broadcasted_iota(jnp.int32, scores.shape, 0)
            col = lax.broadcasted_iota(jnp.int32, scores.shape, 1)
            scores = jnp.where(col <= row, scores, -1e30)
        new_top = jnp.maximum(top, jnp.max(scores, axis=-1, keepdims=True))
        weights = jnp.exp(scores - new_top).astype(BF16)
        total = total * jnp.exp(top - new_top) + plain_dot(weights, v_part[pl.ds(start, block), :])
        return new_top, total

    def both(j, state, masked):
        start = pl.multiple_of(j * block, block)
        top_a, sum_a, top_b, sum_b = state
        top_a, sum_a = one_head(q_first, v_first, start, masked, top_a, sum_a)
        top_b, sum_b = one_head(q_second, v_second, start, masked, top_b, sum_b)
        return top_a, sum_a, top_b, sum_b

    low = jnp.full((block, 1), -1e30, F32)
    zero = jnp.zeros((block, PAIR), F32)
    state = both(at, (low, zero, low, zero), True)
    state = lax.fori_loop(0, at, lambda j, s: both(j, s, False), state)
    top_a, sum_a, top_b, sum_b = state
    mixed = jnp.where(first, sum_a, sum_b)
    total = jnp.where(first, pltpu.roll(sum_a, HD, 1), pltpu.roll(sum_b, HD, 1))
    o_ref[...] = (mixed / total).astype(BF16)
    lse_ref[...] = jnp.where(first, top_a, top_b) + jnp.log(total)


def attend(qkv, block=512):
    length, width3 = qkv.shape
    width = width3 // 3
    pairs = width // PAIR
    steps = length // block
    return pl.pallas_call(
        functools.partial(forward_kernel, block),
        name="attend",
        grid=(pairs, steps),
        in_specs=[
            pl.BlockSpec((block, PAIR), lambda h, i: (i, 3 * h)),
            pl.BlockSpec((length, PAIR), lambda h, i: (0, 3 * h + 1)),
            pl.BlockSpec((length, PAIR), lambda h, i: (0, 3 * h + 2)),
        ],
        out_specs=[
            pl.BlockSpec((block, PAIR), lambda h, i: (i, h)),
            pl.BlockSpec((block, PAIR), lambda h, i: (i, h)),
        ],
        out_shape=[
            jax.ShapeDtypeStruct((length, width), BF16),
            jax.ShapeDtypeStruct((length, width), F32),
        ],
        scratch_shapes=[pltpu.VMEM((length, PAIR), BF16), pltpu.VMEM((length, PAIR), BF16)],
        cost_estimate=pl.CostEstimate(
            flops=8 * length * length * width, bytes_accessed=12 * length * width, transcendentals=length * length * width // HD
        ),
    )(qkv, qkv, qkv)


def backward_kernel(
    block, q_ref, k_ref, v_ref, o_ref, do_ref, lse_ref, cos_ref, sin_ref,
    grad_ref, q_a, q_b, k_a, k_b, do_a, do_b, top_row, dot_row, dq_sum,
):
    length = q_ref.shape[0]
    steps = length // block
    lane = lax.broadcasted_iota(jnp.int32, (1, PAIR), 1)
    first = lane < HD
    ones = jnp.ones((8, PAIR), BF16)
    for i in range(steps):
        at = pl.ds(i * block, block)
        nil = jnp.zeros((block, PAIR), BF16)
        for source, left, right in ((q_ref, q_a, q_b), (k_ref, k_a, k_b), (do_ref, do_a, do_b)):
            values = source[at, :]
            left[at, :] = jnp.where(first, values, nil)
            right[at, :] = jnp.where(first, nil, values)
        product = do_ref[at, :].astype(F32) * o_ref[at, :].astype(F32)
        high_part = product.astype(BF16)
        low_part = (product - high_part.astype(F32)).astype(BF16)
        for slot, keep in ((0, first), (1, jnp.logical_not(first))):
            dot_row[8 * slot : 8 * slot + 8, at] = contract_last(
                ones, jnp.where(keep, high_part, nil)
            ) + contract_last(ones, jnp.where(keep, low_part, nil))
        turned = jnp.transpose(lse_ref[at, :])
        top_row[0:8, at] = turned[0:8, :]
        top_row[8:16, at] = turned[HD : HD + 8, :]
    dq_sum[...] = jnp.zeros_like(dq_sum)

    def one_block(i, j, key_sum, value_sum, masked):
        q_at = pl.ds(pl.multiple_of(i * block, block), block)
        k_at = pl.ds(pl.multiple_of(j * block, block), block)
        keys = k_ref[k_at, :]
        values = v_ref[k_at, :]
        for slot, q_s, k_s, do_s in ((0, q_a, k_a, do_a), (1, q_b, k_b, do_b)):
            q_part = q_s[q_at, :]
            do_part = do_s[q_at, :]
            scores = contract_last(keys, q_part)
            if masked:
                key_at = lax.broadcasted_iota(jnp.int32, scores.shape, 0)
                query_at = lax.broadcasted_iota(jnp.int32, scores.shape, 1)
                scores = jnp.where(key_at <= query_at, scores, -1e30)
            soft = jnp.exp(scores - top_row[8 * slot : 8 * slot + 1, q_at])
            value_sum = value_sum + plain_dot(soft.astype(BF16), do_part)
            grad = contract_last(values, do_part)
            grad_scores = (soft * (grad - dot_row[8 * slot : 8 * slot + 1, q_at])).astype(BF16)
            key_sum = key_sum + plain_dot(grad_scores, q_part)
            dq_sum[q_at, :] += contract_first(grad_scores, k_s[k_at, :])
        return key_sum, value_sum

    def key_block(j, carry):
        zero = jnp.zeros((block, PAIR), F32)
        state = one_block(j, j, zero, zero, True)
        state = lax.fori_loop(j + 1, steps, lambda i, s: one_block(i, j, s[0], s[1], False), state)
        k_at = pl.ds(pl.multiple_of(j * block, block), block)
        grad_ref[k_at, PAIR : 2 * PAIR] = turn(state[0], cos_ref[k_at, :], -sin_ref[k_at, :]).astype(BF16)
        grad_ref[k_at, 2 * PAIR :] = state[1].astype(BF16)
        return carry

    lax.fori_loop(0, steps, key_block, 0)
    for i in range(steps):
        at = pl.ds(i * block, block)
        turned = turn(dq_sum[at, :] * HD**-0.5, cos_ref[at, :], -sin_ref[at, :])
        grad_ref[at, :PAIR] = turned.astype(BF16)


def attend_back(qkv, context, grad_context, lse, tables, pair, block=512):
    length = qkv.shape[0]
    col = lambda at: pl.BlockSpec((length, PAIR), lambda h: (0, at))
    whole = pl.BlockSpec((length, PAIR), lambda h: (0, 0))
    return pl.pallas_call(
        functools.partial(backward_kernel, block),
        name="attend_back",
        grid=(1,),
        in_specs=[col(3 * pair), col(3 * pair + 1), col(3 * pair + 2), col(pair), col(pair), col(pair), whole, whole],
        out_specs=pl.BlockSpec((length, 3 * PAIR), lambda h: (0, 0)),
        out_shape=jax.ShapeDtypeStruct((length, 3 * PAIR), BF16),
        scratch_shapes=[pltpu.VMEM((length, PAIR), BF16)] * 6
        + [pltpu.VMEM((16, length), F32)] * 2
        + [pltpu.VMEM((length, PAIR), F32)],
        cost_estimate=pl.CostEstimate(
            flops=20 * length * length * PAIR, bytes_accessed=20 * length * PAIR, transcendentals=2 * length * length
        ),
    )(qkv, qkv, qkv, context, grad_context, lse, *tables)


def mlp_kernel(
    count, me, x0, x1, x2, x3, g0, g1, g2, g3, gain_ref, down_ref, up_ref,
    n_ref, act_ref, gh_ref, g_ref, part_ref, below_ref, x_held, g_held,
):
    gain = gain_ref[...]
    normed = normalize(take_piece((x0, x1, x2, x3), x_held, count).astype(F32), gain)
    n_ref[...] = normed
    upstream = take_piece((g0, g1, g2, g3), g_held, count)
    g_ref[...] = upstream
    down = down_ref[...]
    up = up_ref[...]
    hidden = plain_dot(normed, up)
    back = contract_last(upstream, down)
    below = 0.5 + 0.5 * lax.erf(hidden * (0.5**0.5))
    activated = (hidden * below).astype(BF16)
    slope = below + hidden * jnp.exp(-0.5 * hidden * hidden) * 0.3989422804014327
    grad_hidden = (back * slope).astype(BF16)
    act_ref[...] = activated
    gh_ref[...] = grad_hidden
    part_ref[...] = plain_dot(activated, down).astype(BF16)
    below_ref[...] = (contract_last(grad_hidden, up) * gain).astype(BF16)


def mlp(me, pieces, grad_pieces, gain_mlp, w_down, w_up, block=256):
    tokens, dim = pieces[0].shape
    length = 4 * tokens
    hid = w_up.shape[1]
    count = tokens // block
    whole = lambda i, me: (0, 0)
    part = lambda i, me: (place(i, me, count), 0)
    tile = lambda columns: pl.BlockSpec((block, columns), part)
    shape = lambda columns: jax.ShapeDtypeStruct((length, columns), BF16)
    return pl.pallas_call(
        functools.partial(mlp_kernel, count),
        name="mlp",
        grid_spec=pltpu.PrefetchScalarGridSpec(
            num_scalar_prefetch=1,
            grid=(length // block,),
            in_specs=piece_specs(pieces, block)
            + piece_specs(grad_pieces, block)
            + [
                pl.BlockSpec((1, dim), whole),
                pl.BlockSpec((hid, dim), whole),
                pl.BlockSpec((dim, hid), whole),
            ],
            out_specs=[tile(dim), tile(hid), tile(hid), tile(dim), tile(dim), tile(dim)],
            scratch_shapes=[
                pltpu.VMEM((block, dim), BF16),
                pltpu.VMEM((block, dim), BF16),
            ],
        ),
        out_shape=[shape(dim), shape(hid), shape(hid), shape(dim), shape(dim), shape(dim)],
        cost_estimate=pl.CostEstimate(
            flops=8 * length * dim * hid, bytes_accessed=16 * length * dim + 4 * dim * hid, transcendentals=2 * length * hid
        ),
    )(me, *pieces, *grad_pieces, gain_mlp, w_down, w_up)


def below_kernel(first_ref, second_ref, w_ref, gain_ref, term_ref, o_ref):
    half = first_ref.shape[1]
    grad = contract_last(first_ref[...], w_ref[:, :half]) + contract_last(second_ref[...], w_ref[:, half:])
    o_ref[...] = (grad * gain_ref[...] + term_ref[...].astype(F32)).astype(BF16)


def below(first, second, weight, gain, term, block=512):
    length, half = first.shape
    dim = weight.shape[0]
    part = lambda i: (i, 0)
    whole = lambda i: (0, 0)
    return pl.pallas_call(
        below_kernel,
        name="below",
        grid=(length // block,),
        in_specs=[
            pl.BlockSpec((block, half), part),
            pl.BlockSpec((block, half), part),
            pl.BlockSpec((dim, 2 * half), whole),
            pl.BlockSpec((1, dim), whole),
            pl.BlockSpec((block, dim), part),
        ],
        out_specs=pl.BlockSpec((block, dim), part),
        out_shape=jax.ShapeDtypeStruct((length, dim), BF16),
        cost_estimate=pl.CostEstimate(
            flops=4 * length * dim * half, bytes_accessed=4 * length * dim + 4 * length * half, transcendentals=0
        ),
    )(first, second, weight, gain, term)


def swap(values, axis, bit):
    ways = lax.axis_size(axis)
    return lax.ppermute(values, axis, [(i, i ^ bit) for i in range(ways)])


def bits_of(ways):
    return [1 << k for k in range(ways.bit_length() - 1)]


def bit_set(axis, bit):
    return (lax.axis_index(axis) & bit) != 0


def pick(values, at, axis):
    return lax.dynamic_index_in_dim(values, at, axis, keepdims=False)


def gather_far_first(shard, axis, at):
    held = shard
    for bit in reversed(bits_of(lax.axis_size(axis))):
        other = swap(held, axis, bit)
        upper = bit_set(axis, bit)
        held = jnp.stack([jnp.where(upper, other, held), jnp.where(upper, held, other)], axis=at)
        at += 1
    return held


def reduce_near_first(values, axis, at):
    bits = bits_of(lax.axis_size(axis))
    held = values.reshape(values.shape[:at] + (2,) * len(bits) + values.shape[at + 1 :])
    for bit in bits:
        mine = (lax.axis_index(axis) & bit) // bit
        spot = at + len(bits) - bits.index(bit) - 1
        arrived = swap(pick(held, 1 - mine, spot), axis, bit)
        held = (pick(held, mine, spot).astype(F32) + arrived.astype(F32)).astype(BF16)
    return held


def exchange(values, axis):
    ways = lax.axis_size(axis)
    me = lax.axis_index(axis)
    pieces = [pick(values, me, 0)]
    for k in range(1, ways):
        pieces.append(swap(pick(values, me ^ k, 0), axis, k))
    count = len(bits_of(ways))
    held = jnp.stack(pieces).reshape((2,) * count + pieces[0].shape)
    for spot, bit in enumerate(reversed(bits_of(ways))):
        held = jnp.where(bit_set(axis, bit), jnp.flip(held, spot), held)
    return held.reshape((ways,) + pieces[0].shape)


def gather_sequence(rows):
    near = swap(rows, "seq", 1)
    far = swap(rows, "seq", 2)
    return rows, near, far, swap(far, "seq", 1)


def sum_sequence(partial):
    me = lax.axis_index("seq")
    tokens = partial.shape[0] // 4
    held = partial.reshape(2, 2, tokens, partial.shape[1])
    mine = me & 1
    arrived = swap(pick(held, 1 - mine, 1), "seq", 1)
    held = (pick(held, mine, 1).astype(F32) + arrived.astype(F32)).astype(BF16)
    mine = me >> 1
    arrived = swap(pick(held, 1 - mine, 0), "seq", 2)
    return pick(held, mine, 0).astype(F32) + arrived.astype(F32)


def rotary_tables(length):
    lane = jnp.arange(PAIR, dtype=jnp.int32) % HD
    step = (lane % (ROT // 2)).astype(F32)
    frequency = jnp.where(lane < ROT, 10000.0 ** (-(step * 2.0) / ROT), 0.0)
    angles = jnp.arange(length, dtype=jnp.int32).astype(F32)[:, None] * frequency[None, :]
    return jnp.cos(angles), jnp.sin(angles)


def adam_step(weight, gradient, moment, square, decay_rate):
    moment_next = BETA_ONE * moment + (1.0 - BETA_ONE) * gradient
    square_next = BETA_TWO * square + (1.0 - BETA_TWO) * gradient * gradient
    moment_hat = moment_next / (1.0 - BETA_ONE**STEP)
    square_hat = square_next / (1.0 - BETA_TWO**STEP)
    change = -RATE * (
        moment_hat / (jnp.sqrt(square_hat) + ADAM_EPS) + decay_rate * weight.astype(F32)
    )
    return (moment_next, square_next, change)


def one_step(
    layer_input, w_qkv, w_out, w_up, w_down, gain_attn, gain_mlp, out_grad,
    moment_qkv, square_qkv, moment_out, square_out, moment_up, square_up, moment_down, square_down,
    moment_gattn, square_gattn, moment_gmlp, square_gmlp,
):
    ways = lax.axis_size("seq")
    fold = lax.axis_size("fsdp")
    rows = w_qkv.shape[0]
    dim = rows * ways * fold
    inner = w_qkv.shape[1] // 3
    group = inner // ways
    hid = w_up.shape[1] // ways
    tokens = layer_input.shape[1]
    length = tokens * ways

    me = lax.axis_index("seq").astype(jnp.int32).reshape(1)
    gains = gather_far_first(
        gather_far_first(jnp.stack([gain_attn, gain_mlp]), "seq", 1), "fsdp", 3
    ).reshape(2, dim).astype(F32)
    down_rows = w_down.shape[0]
    split_up = w_up.reshape(rows, ways, hid).transpose(1, 0, 2)
    full_down = lax.all_gather(w_down, "fsdp", tiled=True)
    local_up = exchange(split_up, "seq")
    full_up = gather_far_first(local_up, "fsdp", 1).reshape(dim, hid)
    local_rows = layer_input[0]
    row_pieces = gather_sequence(local_rows)
    grad_pieces = gather_sequence(out_grad[0])
    count = group // PAIR
    split_qkv = (
        w_qkv.reshape(rows, 3, ways, count, PAIR).transpose(2, 0, 3, 1, 4).reshape(ways, rows, 3 * group)
    )
    local_qkv = exchange(split_qkv, "seq")
    flat_out = w_out.reshape(rows, ways, dim // ways).transpose(1, 0, 2)
    both = lax.all_gather(jnp.concatenate([local_qkv, flat_out], axis=2), "fsdp")
    full_qkv = both[..., : 3 * group].transpose(1, 0, 2, 3).reshape(dim, 3 * group)
    full_out = both[..., 3 * group :].transpose(0, 2, 1, 3).reshape(fold * rows, dim)
    tables = rotary_tables(length)
    gains, tables = lax.optimization_barrier((gains, tables))

    normed_mlp, activated, grad_hidden, upstream, partial, mlp_term = mlp(
        me, row_pieces, grad_pieces, gains[1:2], full_down, full_up
    )
    grad_wdown = contract_first(activated, upstream).astype(BF16)
    grad_wup = contract_first(normed_mlp, grad_hidden).astype(BF16)
    sendable = jnp.concatenate(
        [
            grad_wdown.reshape(fold, down_rows, dim),
            grad_wup.reshape(ways, fold, rows, hid).transpose(1, 0, 2, 3).reshape(fold, ways * rows, hid),
        ],
        axis=1,
    )
    sendable, full_qkv = lax.optimization_barrier((sendable, full_qkv))
    owned_sum = lax.psum_scatter(sendable, "fsdp", scatter_dimension=0)

    normed_attn, qkv = project(me, row_pieces, gains[0:1], full_qkv, tables)
    context, lse = attend(qkv)
    grad_context = contract_last(upstream, full_out).astype(BF16)
    partial = (plain_dot(context, full_out) + partial.astype(F32)).astype(BF16)
    grad_wout = contract_first(context, upstream).astype(BF16)
    grad_context, partial, grad_wout = lax.optimization_barrier((grad_context, partial, grad_wout))
    branch = sum_sequence(partial)
    layer_output = (local_rows.astype(F32) + branch).astype(BF16)[None]
    sum_out = reduce_near_first(grad_wout.reshape(fold, rows, dim), "fsdp", 0).astype(F32)

    near_pairs = []
    grad_pairs = []
    for pair in range(count):
        grad_pair = attend_back(qkv, context, grad_context, lse, tables, pair)
        if pair + 1 == count:
            grad_pair, owned_sum = lax.optimization_barrier((grad_pair, owned_sum))
        grad_weight = contract_first(normed_attn, grad_pair).astype(BF16)
        if pair + 1 < count:
            grad_weight, grad_context = lax.optimization_barrier((grad_weight, grad_context))
        near = reduce_near_first(grad_weight.reshape(ways, fold, rows, 3 * PAIR), "fsdp", 1)
        near_pairs.append(near)
        grad_pairs.append(grad_pair)
    upper = below(grad_pairs[0], grad_pairs[1], full_qkv, gains[0:1], mlp_term)
    sum_down = owned_sum[:down_rows].astype(F32)
    back_up = exchange(owned_sum[down_rows:].reshape(ways, rows, hid), "seq")
    sum_up = back_up.transpose(1, 0, 2).reshape(rows, ways * hid).astype(F32)
    near_qkv = jnp.concatenate(near_pairs, axis=2)
    back_qkv = exchange(near_qkv, "seq")
    sum_qkv = (
        back_qkv.reshape(ways, rows, count, 3, PAIR).transpose(1, 3, 0, 2, 4).reshape(rows, 3 * inner).astype(F32)
    )

    upper = sum_sequence(upper)
    local = local_rows.astype(F32)
    centred = local - jnp.mean(local, axis=-1, keepdims=True)
    inverse = lax.rsqrt(jnp.mean(centred * centred, axis=-1, keepdims=True) + EPS_NORM)
    xhat = centred * inverse
    term = inverse * (
        upper
        - jnp.mean(upper, axis=-1, keepdims=True)
        - xhat * jnp.mean(upper * xhat, axis=-1, keepdims=True)
    )
    input_grad = (out_grad[0].astype(F32) + term).astype(BF16)[None]

    sum_gattn = jnp.sum(w_qkv.astype(F32) * sum_qkv, axis=1) / gain_attn.astype(F32)
    sum_gmlp = jnp.sum(w_up.astype(F32) * sum_up, axis=1) / gain_mlp.astype(F32)
    summed = (sum_qkv, sum_out, sum_up, sum_down, sum_gattn, sum_gmlp)
    owned = (w_qkv, w_out, w_up, w_down, gain_attn, gain_mlp)
    moments = (moment_qkv, moment_out, moment_up, moment_down, moment_gattn, moment_gmlp)
    squares = (square_qkv, square_out, square_up, square_down, square_gattn, square_gmlp)
    decays = (DECAY, DECAY, DECAY, DECAY, 0.0, 0.0)
    results = [
        adam_step(owned[slot], summed[slot], moments[slot], squares[slot], decays[slot])
        for slot in range(6)
    ]
    return (
        (layer_output, input_grad)
        + summed
        + tuple(result[0] for result in results)
        + tuple(result[1] for result in results)
        + tuple(result[2] for result in results)
    )


def solution(mesh):
    acts = P("fsdp", "seq", None)
    mat = P(("seq", "fsdp"), None)
    vec = P(("seq", "fsdp"))
    six = (mat, mat, mat, mat, vec, vec)
    return jax.shard_map(
        one_step,
        mesh=mesh,
        in_specs=(acts,) + six + (acts,) + (mat,) * 8 + (vec,) * 4,
        out_specs=(acts, acts) + six * 4,
        check_vma=False,
    )
```

```python
import functools
import jax
import jax.numpy as jnp
from jax import lax
from jax.experimental import pallas as pl
from jax.experimental.pallas import tpu as pltpu
from jax.sharding import PartitionSpec as P


F32 = jnp.float32
BF16 = jnp.bfloat16
EPS_NORM = 1e-05
HD = 64
ROT = 16
PAIR = 2 * HD
STEP = 10
BETA_ONE = 0.9
BETA_TWO = 0.95
RATE = 0.02
DECAY = 0.1
ADAM_EPS = 1e-08


def contract_last(left, right):
    return lax.dot_general(left, right, (((1,), (1,)), ((), ())), preferred_element_type=F32)


def contract_first(left, right):
    return lax.dot_general(left, right, (((0,), (0,)), ((), ())), preferred_element_type=F32)


def plain_dot(left, right):
    return lax.dot_general(left, right, (((1,), (0,)), ((), ())), preferred_element_type=F32)


def turn(pair_values, cosine, sine):
    lane = lax.broadcasted_iota(jnp.int32, (1, PAIR), 1)
    ahead = pltpu.roll(pair_values, PAIR - ROT // 2, 1)
    behind = pltpu.roll(pair_values, ROT // 2, 1)
    return pair_values * cosine + jnp.where(lane % HD < ROT // 2, -ahead, behind) * sine


def place(i, me, count):
    return ((i // count) ^ me[0]) * count + i % count


def piece_specs(pieces, block):
    count = pieces[0].shape[0] // block

    def spec(k):
        return pl.BlockSpec(
            (block, pieces[0].shape[1]), lambda i, me: (jnp.clip(i - k * count, 0, count - 1), 0)
        )

    return [spec(k) for k in range(len(pieces))]


def take_piece(refs, held, count):
    step = pl.program_id(0)
    for k, ref in enumerate(refs):

        @pl.when(step // count == k)
        def _():
            held[...] = ref[...]

    return held[...]


def normalize(rows, gain):
    centred = rows - jnp.mean(rows, axis=-1, keepdims=True)
    spread = jnp.mean(centred * centred, axis=-1, keepdims=True)
    return (centred * lax.rsqrt(spread + EPS_NORM) * gain).astype(BF16)


def project_kernel(count, me, x0, x1, x2, x3, ga_ref, w_ref, cos_ref, sin_ref, na_ref, qkv_ref, held):
    rows = take_piece((x0, x1, x2, x3), held, count).astype(F32)
    normed = normalize(rows, ga_ref[...])
    na_ref[...] = normed
    projected = plain_dot(normed, w_ref[...])
    width = w_ref.shape[1] // 3
    cosine = cos_ref[...]
    sine = sin_ref[...]
    for start in range(0, 3 * width, PAIR):
        columns = projected[:, start : start + PAIR]
        kind = start // PAIR % 3
        if kind < 2:
            columns = turn(columns, cosine, sine)
        columns = columns.astype(BF16)
        if kind == 0:
            columns = columns * jnp.asarray(HD**-0.5, BF16)
        qkv_ref[:, start : start + PAIR] = columns


def project(me, pieces, gain_attn, weight, tables, block=256):
    tokens, dim = pieces[0].shape
    count = tokens // block
    length = 4 * tokens
    width = weight.shape[1]
    whole = lambda i, me: (0, 0)
    part = lambda i, me: (place(i, me, count), 0)
    return pl.pallas_call(
        functools.partial(project_kernel, count),
        name="project",
        grid_spec=pltpu.PrefetchScalarGridSpec(
            num_scalar_prefetch=1,
            grid=(length // block,),
            in_specs=piece_specs(pieces, block)
            + [
                pl.BlockSpec((1, dim), whole),
                pl.BlockSpec((dim, width), whole),
                pl.BlockSpec((block, PAIR), part),
                pl.BlockSpec((block, PAIR), part),
            ],
            out_specs=[
                pl.BlockSpec((block, dim), part),
                pl.BlockSpec((block, width), part),
            ],
            scratch_shapes=[pltpu.VMEM((block, dim), BF16)],
        ),
        out_shape=[
            jax.ShapeDtypeStruct((length, dim), BF16),
            jax.ShapeDtypeStruct((length, width), BF16),
        ],
        cost_estimate=pl.CostEstimate(
            flops=2 * length * dim * width, bytes_accessed=6 * length * dim + 2 * length * width, transcendentals=0
        ),
    )(me, *pieces, gain_attn, weight, *tables)


def forward_kernel(block, q_ref, k_ref, v_ref, o_ref, lse_ref, v_first, v_second):
    at = pl.program_id(1)
    lane = lax.broadcasted_iota(jnp.int32, (1, PAIR), 1)
    first = lane < HD

    @pl.when(at == 0)
    def _():
        values = v_ref[...]
        one = jnp.ones_like(values)
        v_first[...] = jnp.where(first, values, one)
        v_second[...] = jnp.where(first, one, values)

    queries = q_ref[...]
    nil = jnp.zeros_like(queries)
    q_first = jnp.where(first, queries, nil)
    q_second = jnp.where(first, nil, queries)

    def one_head(q_part, v_part, start, masked, top, total):
        keys = k_ref[pl.ds(start, block), :]
        scores = contract_last(q_part, keys)
        if masked:
            row = lax.broadcasted_iota(jnp.int32, scores.shape, 0)
            col = lax.broadcasted_iota(jnp.int32, scores.shape, 1)
            scores = jnp.where(col <= row, scores, -1e30)
        new_top = jnp.maximum(top, jnp.max(scores, axis=-1, keepdims=True))
        weights = jnp.exp(scores - new_top).astype(BF16)
        total = total * jnp.exp(top - new_top) + plain_dot(weights, v_part[pl.ds(start, block), :])
        return new_top, total

    def both(j, state, masked):
        start = pl.multiple_of(j * block, block)
        top_a, sum_a, top_b, sum_b = state
        top_a, sum_a = one_head(q_first, v_first, start, masked, top_a, sum_a)
        top_b, sum_b = one_head(q_second, v_second, start, masked, top_b, sum_b)
        return top_a, sum_a, top_b, sum_b

    low = jnp.full((block, 1), -1e30, F32)
    zero = jnp.zeros((block, PAIR), F32)
    state = both(at, (low, zero, low, zero), True)
    state = lax.fori_loop(0, at, lambda j, s: both(j, s, False), state)
    top_a, sum_a, top_b, sum_b = state
    mixed = jnp.where(first, sum_a, sum_b)
    total = jnp.where(first, pltpu.roll(sum_a, HD, 1), pltpu.roll(sum_b, HD, 1))
    o_ref[...] = (mixed / total).astype(BF16)
    lse_ref[...] = jnp.where(first, top_a, top_b) + jnp.log(total)


def attend(qkv, block=512):
    length, width3 = qkv.shape
    width = width3 // 3
    pairs = width // PAIR
    steps = length // block
    return pl.pallas_call(
        functools.partial(forward_kernel, block),
        name="attend",
        grid=(pairs, steps),
        in_specs=[
            pl.BlockSpec((block, PAIR), lambda h, i: (i, 3 * h)),
            pl.BlockSpec((length, PAIR), lambda h, i: (0, 3 * h + 1)),
            pl.BlockSpec((length, PAIR), lambda h, i: (0, 3 * h + 2)),
        ],
        out_specs=[
            pl.BlockSpec((block, PAIR), lambda h, i: (i, h)),
            pl.BlockSpec((block, PAIR), lambda h, i: (i, h)),
        ],
        out_shape=[
            jax.ShapeDtypeStruct((length, width), BF16),
            jax.ShapeDtypeStruct((length, width), F32),
        ],
        scratch_shapes=[pltpu.VMEM((length, PAIR), BF16), pltpu.VMEM((length, PAIR), BF16)],
        cost_estimate=pl.CostEstimate(
            flops=8 * length * length * width, bytes_accessed=12 * length * width, transcendentals=length * length * width // HD
        ),
    )(qkv, qkv, qkv)


def backward_kernel(
    block, q_ref, k_ref, v_ref, o_ref, do_ref, lse_ref, cos_ref, sin_ref,
    grad_ref, q_a, q_b, k_a, k_b, do_a, do_b, top_row, dot_row, dq_sum,
):
    length = q_ref.shape[0]
    steps = length // block
    lane = lax.broadcasted_iota(jnp.int32, (1, PAIR), 1)
    first = lane < HD
    ones = jnp.ones((8, PAIR), BF16)
    for i in range(steps):
        at = pl.ds(i * block, block)
        nil = jnp.zeros((block, PAIR), BF16)
        for source, left, right in ((q_ref, q_a, q_b), (k_ref, k_a, k_b), (do_ref, do_a, do_b)):
            values = source[at, :]
            left[at, :] = jnp.where(first, values, nil)
            right[at, :] = jnp.where(first, nil, values)
        product = do_ref[at, :].astype(F32) * o_ref[at, :].astype(F32)
        high_part = product.astype(BF16)
        low_part = (product - high_part.astype(F32)).astype(BF16)
        for slot, keep in ((0, first), (1, jnp.logical_not(first))):
            dot_row[8 * slot : 8 * slot + 8, at] = contract_last(
                ones, jnp.where(keep, high_part, nil)
            ) + contract_last(ones, jnp.where(keep, low_part, nil))
        turned = jnp.transpose(lse_ref[at, :])
        top_row[0:8, at] = turned[0:8, :]
        top_row[8:16, at] = turned[HD : HD + 8, :]
    dq_sum[...] = jnp.zeros_like(dq_sum)

    def one_block(i, j, key_sum, value_sum, masked):
        q_at = pl.ds(pl.multiple_of(i * block, block), block)
        k_at = pl.ds(pl.multiple_of(j * block, block), block)
        keys = k_ref[k_at, :]
        values = v_ref[k_at, :]
        for slot, q_s, k_s, do_s in ((0, q_a, k_a, do_a), (1, q_b, k_b, do_b)):
            q_part = q_s[q_at, :]
            do_part = do_s[q_at, :]
            scores = contract_last(keys, q_part)
            if masked:
                key_at = lax.broadcasted_iota(jnp.int32, scores.shape, 0)
                query_at = lax.broadcasted_iota(jnp.int32, scores.shape, 1)
                scores = jnp.where(key_at <= query_at, scores, -1e30)
            soft = jnp.exp(scores - top_row[8 * slot : 8 * slot + 1, q_at])
            value_sum = value_sum + plain_dot(soft.astype(BF16), do_part)
            grad = contract_last(values, do_part)
            grad_scores = (soft * (grad - dot_row[8 * slot : 8 * slot + 1, q_at])).astype(BF16)
            key_sum = key_sum + plain_dot(grad_scores, q_part)
            dq_sum[q_at, :] += contract_first(grad_scores, k_s[k_at, :])
        return key_sum, value_sum

    def key_block(j, carry):
        zero = jnp.zeros((block, PAIR), F32)
        state = one_block(j, j, zero, zero, True)
        state = lax.fori_loop(j + 1, steps, lambda i, s: one_block(i, j, s[0], s[1], False), state)
        k_at = pl.ds(pl.multiple_of(j * block, block), block)
        grad_ref[k_at, PAIR : 2 * PAIR] = turn(state[0], cos_ref[k_at, :], -sin_ref[k_at, :]).astype(BF16)
        grad_ref[k_at, 2 * PAIR :] = state[1].astype(BF16)
        return carry

    lax.fori_loop(0, steps, key_block, 0)
    for i in range(steps):
        at = pl.ds(i * block, block)
        turned = turn(dq_sum[at, :] * HD**-0.5, cos_ref[at, :], -sin_ref[at, :])
        grad_ref[at, :PAIR] = turned.astype(BF16)


def attend_back(qkv, context, grad_context, lse, tables, pair, block=512):
    length = qkv.shape[0]
    col = lambda at: pl.BlockSpec((length, PAIR), lambda h: (0, at))
    whole = pl.BlockSpec((length, PAIR), lambda h: (0, 0))
    return pl.pallas_call(
        functools.partial(backward_kernel, block),
        name="attend_back",
        grid=(1,),
        in_specs=[col(3 * pair), col(3 * pair + 1), col(3 * pair + 2), col(pair), col(pair), col(pair), whole, whole],
        out_specs=pl.BlockSpec((length, 3 * PAIR), lambda h: (0, 0)),
        out_shape=jax.ShapeDtypeStruct((length, 3 * PAIR), BF16),
        scratch_shapes=[pltpu.VMEM((length, PAIR), BF16)] * 6
        + [pltpu.VMEM((16, length), F32)] * 2
        + [pltpu.VMEM((length, PAIR), F32)],
        cost_estimate=pl.CostEstimate(
            flops=20 * length * length * PAIR, bytes_accessed=20 * length * PAIR, transcendentals=2 * length * length
        ),
    )(qkv, qkv, qkv, context, grad_context, lse, *tables)


def feed_core(normed, upstream, gain, down_ref, up_ref, act_ref, gh_ref):
    down = down_ref[...]
    up = up_ref[...]
    hidden = plain_dot(normed, up)
    back = contract_last(upstream, down)
    under = 0.5 + 0.5 * lax.erf(hidden * (0.5**0.5))
    activated = (hidden * under).astype(BF16)
    slope = under + hidden * jnp.exp(-0.5 * hidden * hidden) * 0.3989422804014327
    grad_hidden = (back * slope).astype(BF16)
    act_ref[...] = activated
    gh_ref[...] = grad_hidden
    return plain_dot(activated, down), contract_last(grad_hidden, up) * gain


def second_kernel(n_ref, g_ref, part_in, term_in, gain_ref, down_ref, up_ref, act_ref, gh_ref, part_ref, below_ref):
    part, term = feed_core(n_ref[...], g_ref[...], gain_ref[...], down_ref, up_ref, act_ref, gh_ref)
    part_ref[...] = (part + part_in[...].astype(F32)).astype(BF16)
    below_ref[...] = (term + term_in[...].astype(F32)).astype(BF16)


def mlp_second(normed, upstream, partial, term, gain_mlp, w_down, w_up, block=256):
    length, dim = normed.shape
    hid = w_up.shape[1]
    whole = lambda i: (0, 0)
    tile = lambda columns: pl.BlockSpec((block, columns), lambda i: (i, 0))
    shape = lambda columns: jax.ShapeDtypeStruct((length, columns), BF16)
    return pl.pallas_call(
        second_kernel,
        name="mlp_second",
        grid=(length // block,),
        in_specs=[
            tile(dim), tile(dim), tile(dim), tile(dim),
            pl.BlockSpec((1, dim), whole),
            pl.BlockSpec((hid, dim), whole),
            pl.BlockSpec((dim, hid), whole),
        ],
        out_specs=[tile(hid), tile(hid), tile(dim), tile(dim)],
        out_shape=[shape(hid), shape(hid), shape(dim), shape(dim)],
        cost_estimate=pl.CostEstimate(
            flops=8 * length * dim * hid, bytes_accessed=16 * length * dim + 4 * dim * hid, transcendentals=2 * length * hid
        ),
    )(normed, upstream, partial, term, gain_mlp, w_down, w_up)


def mlp_kernel(
    count, me, x0, x1, x2, x3, g0, g1, g2, g3, gain_ref, down_ref, up_ref,
    n_ref, act_ref, gh_ref, g_ref, part_ref, below_ref, x_held, g_held,
):
    gain = gain_ref[...]
    normed = normalize(take_piece((x0, x1, x2, x3), x_held, count).astype(F32), gain)
    n_ref[...] = normed
    upstream = take_piece((g0, g1, g2, g3), g_held, count)
    g_ref[...] = upstream
    part, term = feed_core(normed, upstream, gain, down_ref, up_ref, act_ref, gh_ref)
    part_ref[...] = part.astype(BF16)
    below_ref[...] = term.astype(BF16)


def mlp(me, pieces, grad_pieces, gain_mlp, w_down, w_up, block=256):
    tokens, dim = pieces[0].shape
    length = 4 * tokens
    hid = w_up.shape[1]
    count = tokens // block
    whole = lambda i, me: (0, 0)
    part = lambda i, me: (place(i, me, count), 0)
    tile = lambda columns: pl.BlockSpec((block, columns), part)
    shape = lambda columns: jax.ShapeDtypeStruct((length, columns), BF16)
    return pl.pallas_call(
        functools.partial(mlp_kernel, count),
        name="mlp",
        grid_spec=pltpu.PrefetchScalarGridSpec(
            num_scalar_prefetch=1,
            grid=(length // block,),
            in_specs=piece_specs(pieces, block)
            + piece_specs(grad_pieces, block)
            + [
                pl.BlockSpec((1, dim), whole),
                pl.BlockSpec((hid, dim), whole),
                pl.BlockSpec((dim, hid), whole),
            ],
            out_specs=[tile(dim), tile(hid), tile(hid), tile(dim), tile(dim), tile(dim)],
            scratch_shapes=[
                pltpu.VMEM((block, dim), BF16),
                pltpu.VMEM((block, dim), BF16),
            ],
        ),
        out_shape=[shape(dim), shape(hid), shape(hid), shape(dim), shape(dim), shape(dim)],
        cost_estimate=pl.CostEstimate(
            flops=8 * length * dim * hid, bytes_accessed=16 * length * dim + 4 * dim * hid, transcendentals=2 * length * hid
        ),
    )(me, *pieces, *grad_pieces, gain_mlp, w_down, w_up)


def below_kernel(first_ref, second_ref, w_ref, gain_ref, term_ref, o_ref):
    grad = contract_last(jnp.concatenate([first_ref[...], second_ref[...]], axis=1), w_ref[...])
    o_ref[...] = (grad * gain_ref[...] + term_ref[...].astype(F32)).astype(BF16)


def below(first, second, weight, gain, term, block=512):
    length, half = first.shape
    dim = weight.shape[0]
    part = lambda i: (i, 0)
    whole = lambda i: (0, 0)
    return pl.pallas_call(
        below_kernel,
        name="below",
        grid=(length // block,),
        in_specs=[
            pl.BlockSpec((block, half), part),
            pl.BlockSpec((block, half), part),
            pl.BlockSpec((dim, 2 * half), whole),
            pl.BlockSpec((1, dim), whole),
            pl.BlockSpec((block, dim), part),
        ],
        out_specs=pl.BlockSpec((block, dim), part),
        out_shape=jax.ShapeDtypeStruct((length, dim), BF16),
        cost_estimate=pl.CostEstimate(
            flops=4 * length * dim * half, bytes_accessed=4 * length * dim + 4 * length * half, transcendentals=0
        ),
    )(first, second, weight, gain, term)


def swap(values, axis, bit):
    ways = lax.axis_size(axis)
    return lax.ppermute(values, axis, [(i, i ^ bit) for i in range(ways)])


def bits_of(ways):
    return [1 << k for k in range(ways.bit_length() - 1)]


def bit_set(axis, bit):
    return (lax.axis_index(axis) & bit) != 0


def pick(values, at, axis):
    return lax.dynamic_index_in_dim(values, at, axis, keepdims=False)


def gather_far_first(shard, axis, at):
    held = shard
    for bit in reversed(bits_of(lax.axis_size(axis))):
        other = swap(held, axis, bit)
        upper = bit_set(axis, bit)
        held = jnp.stack([jnp.where(upper, other, held), jnp.where(upper, held, other)], axis=at)
        at += 1
    return held


def reduce_near_first(values, axis, at):
    bits = bits_of(lax.axis_size(axis))
    held = values.reshape(values.shape[:at] + (2,) * len(bits) + values.shape[at + 1 :])
    for bit in bits:
        mine = (lax.axis_index(axis) & bit) // bit
        spot = at + len(bits) - bits.index(bit) - 1
        arrived = swap(pick(held, 1 - mine, spot), axis, bit)
        held = (pick(held, mine, spot).astype(F32) + arrived.astype(F32)).astype(BF16)
    return held


def exchange(values, axis):
    ways = lax.axis_size(axis)
    me = lax.axis_index(axis)
    pieces = [pick(values, me, 0)]
    for k in range(1, ways):
        pieces.append(swap(pick(values, me ^ k, 0), axis, k))
    count = len(bits_of(ways))
    held = jnp.stack(pieces).reshape((2,) * count + pieces[0].shape)
    for spot, bit in enumerate(reversed(bits_of(ways))):
        held = jnp.where(bit_set(axis, bit), jnp.flip(held, spot), held)
    return held.reshape((ways,) + pieces[0].shape)


def gather_sequence(rows):
    near = swap(rows, "seq", 1)
    far = swap(rows, "seq", 2)
    return rows, near, far, swap(far, "seq", 1)


def sum_sequence(partial):
    me = lax.axis_index("seq")
    tokens = partial.shape[0] // 4
    held = partial.reshape(2, 2, tokens, partial.shape[1])
    mine = me & 1
    arrived = swap(pick(held, 1 - mine, 1), "seq", 1)
    held = (pick(held, mine, 1).astype(F32) + arrived.astype(F32)).astype(BF16)
    mine = me >> 1
    arrived = swap(pick(held, 1 - mine, 0), "seq", 2)
    return pick(held, mine, 0).astype(F32) + arrived.astype(F32)


def rotary_tables(length):
    lane = jnp.arange(PAIR, dtype=jnp.int32) % HD
    step = (lane % (ROT // 2)).astype(F32)
    frequency = jnp.where(lane < ROT, 10000.0 ** (-(step * 2.0) / ROT), 0.0)
    angles = jnp.arange(length, dtype=jnp.int32).astype(F32)[:, None] * frequency[None, :]
    return jnp.cos(angles), jnp.sin(angles)


def adam_step(weight, gradient, moment, square, decay_rate):
    moment_next = BETA_ONE * moment + (1.0 - BETA_ONE) * gradient
    square_next = BETA_TWO * square + (1.0 - BETA_TWO) * gradient * gradient
    moment_hat = moment_next / (1.0 - BETA_ONE**STEP)
    square_hat = square_next / (1.0 - BETA_TWO**STEP)
    change = -RATE * (
        moment_hat / (jnp.sqrt(square_hat) + ADAM_EPS) + decay_rate * weight.astype(F32)
    )
    return (moment_next, square_next, change)


def one_step(
    layer_input, w_qkv, w_out, w_up, w_down, gain_attn, gain_mlp, out_grad,
    moment_qkv, square_qkv, moment_out, square_out, moment_up, square_up, moment_down, square_down,
    moment_gattn, square_gattn, moment_gmlp, square_gmlp,
):
    ways = lax.axis_size("seq")
    fold = lax.axis_size("fsdp")
    rows = w_qkv.shape[0]
    dim = rows * ways * fold
    inner = w_qkv.shape[1] // 3
    group = inner // ways
    hid = w_up.shape[1] // ways
    tokens = layer_input.shape[1]
    length = tokens * ways

    me = lax.axis_index("seq").astype(jnp.int32).reshape(1)
    gains = gather_far_first(
        gather_far_first(jnp.stack([gain_attn, gain_mlp]), "seq", 1), "fsdp", 3
    ).reshape(2, dim).astype(F32)
    down_rows = w_down.shape[0]
    half_rows = down_rows // 2
    half = hid // 2
    split_up = (
        w_up.reshape(rows, ways, fold, 2, half_rows).transpose(1, 3, 0, 2, 4).reshape(ways, 2, rows, half)
    )
    local_up = exchange(split_up, "seq")
    local_down = (
        w_down.reshape(2, 2, rows, 2, half).transpose(0, 3, 1, 2, 4).reshape(2, ways, rows, half)
    )
    packed = [jnp.concatenate([local_up[:, k], local_down[k]], axis=1) for k in range(2)]
    first = lax.all_gather(packed[0], "fsdp")
    first = first.transpose(1, 0, 2, 3)
    second = gather_far_first(packed[1], "fsdp", 1).reshape(ways, fold, 2 * rows, half)

    def unpack(both):
        up = both[:, :, :rows].reshape(dim, half)
        down = both[:, :, rows:].reshape(2, 2, fold, rows, half).transpose(2, 1, 3, 0, 4)
        return up, down.reshape(half, dim)

    local_rows = layer_input[0]
    row_pieces = gather_sequence(local_rows)
    grad_pieces = gather_sequence(out_grad[0])
    count = group // PAIR
    split_qkv = (
        w_qkv.reshape(rows, 3, ways, count, PAIR).transpose(2, 0, 3, 1, 4).reshape(ways, rows, 3 * group)
    )
    local_qkv = exchange(split_qkv, "seq")
    flat_out = w_out.reshape(rows, ways, dim // ways).transpose(1, 0, 2)
    both = lax.all_gather(jnp.concatenate([local_qkv, flat_out], axis=2), "fsdp")
    full_qkv = both[..., : 3 * group].transpose(1, 0, 2, 3).reshape(dim, 3 * group)
    full_out = both[..., 3 * group :].transpose(0, 2, 1, 3).reshape(fold * rows, dim)
    tables = rotary_tables(length)
    gains, tables = lax.optimization_barrier((gains, tables))

    up_first, down_first = unpack(first)
    normed_mlp, activated, grad_hidden, upstream, partial, mlp_term = mlp(
        me, row_pieces, grad_pieces, gains[1:2], down_first, up_first
    )

    def feed_gradients(activated, grad_hidden):
        grad_wdown = contract_first(activated, upstream).astype(BF16)
        grad_wup = contract_first(normed_mlp, grad_hidden).astype(BF16)
        return (
            grad_wdown.reshape(fold, half_rows, dim),
            grad_wup.reshape(ways, fold, rows, half).transpose(1, 0, 2, 3).reshape(fold, ways * rows, half),
        )

    grads_first = feed_gradients(activated, grad_hidden)
    up_second, down_second = unpack(second)
    grads_first, partial = lax.optimization_barrier((grads_first, partial))
    activated, grad_hidden, partial, mlp_term = mlp_second(
        normed_mlp, upstream, partial, mlp_term, gains[1:2], down_second, up_second
    )
    grads_second = feed_gradients(activated, grad_hidden)
    sendable = jnp.concatenate(
        [grads_first[0], grads_second[0], jnp.concatenate([grads_first[1], grads_second[1]], axis=2)], axis=1
    )
    sendable, full_qkv = lax.optimization_barrier((sendable, full_qkv))
    owned_sum = lax.psum_scatter(sendable, "fsdp", scatter_dimension=0)

    normed_attn, qkv = project(me, row_pieces, gains[0:1], full_qkv, tables)
    context, lse = attend(qkv)
    grad_context = contract_last(upstream, full_out).astype(BF16)
    partial = (plain_dot(context, full_out) + partial.astype(F32)).astype(BF16)
    grad_wout = contract_first(context, upstream).astype(BF16)
    grad_context, partial, grad_wout = lax.optimization_barrier((grad_context, partial, grad_wout))
    branch = sum_sequence(partial)
    layer_output = (local_rows.astype(F32) + branch).astype(BF16)[None]
    sum_out = reduce_near_first(grad_wout.reshape(fold, rows, dim), "fsdp", 0).astype(F32)

    near_pairs = []
    grad_pairs = []
    for pair in range(count):
        grad_pair = attend_back(qkv, context, grad_context, lse, tables, pair)
        grad_weight = contract_first(normed_attn, grad_pair).astype(BF16)
        if pair + 1 < count:
            grad_weight, grad_context = lax.optimization_barrier((grad_weight, grad_context))
        near = reduce_near_first(grad_weight.reshape(ways, fold, rows, 3 * PAIR), "fsdp", 1)
        near_pairs.append(near)
        grad_pairs.append(grad_pair)
    upper = below(grad_pairs[0], grad_pairs[1], full_qkv, gains[0:1], mlp_term)
    sum_down = owned_sum[:down_rows].astype(F32)
    back_up = exchange(owned_sum[down_rows:].reshape(ways, rows, hid), "seq")
    sum_up = (
        back_up.reshape(ways, rows, 2, fold, half_rows).transpose(1, 0, 3, 2, 4).reshape(rows, ways * hid).astype(F32)
    )
    near_qkv = jnp.concatenate(near_pairs, axis=2)
    back_qkv = exchange(near_qkv, "seq")
    sum_qkv = (
        back_qkv.reshape(ways, rows, count, 3, PAIR).transpose(1, 3, 0, 2, 4).reshape(rows, 3 * inner).astype(F32)
    )

    upper = sum_sequence(upper)
    local = local_rows.astype(F32)
    centred = local - jnp.mean(local, axis=-1, keepdims=True)
    inverse = lax.rsqrt(jnp.mean(centred * centred, axis=-1, keepdims=True) + EPS_NORM)
    xhat = centred * inverse
    term = inverse * (
        upper
        - jnp.mean(upper, axis=-1, keepdims=True)
        - xhat * jnp.mean(upper * xhat, axis=-1, keepdims=True)
    )
    input_grad = (out_grad[0].astype(F32) + term).astype(BF16)[None]

    sum_gattn = jnp.sum(w_qkv.astype(F32) * sum_qkv, axis=1) / gain_attn.astype(F32)
    sum_gmlp = jnp.sum(w_up.astype(F32) * sum_up, axis=1) / gain_mlp.astype(F32)
    summed = (sum_qkv, sum_out, sum_up, sum_down, sum_gattn, sum_gmlp)
    owned = (w_qkv, w_out, w_up, w_down, gain_attn, gain_mlp)
    moments = (moment_qkv, moment_out, moment_up, moment_down, moment_gattn, moment_gmlp)
    squares = (square_qkv, square_out, square_up, square_down, square_gattn, square_gmlp)
    decays = (DECAY, DECAY, DECAY, DECAY, 0.0, 0.0)
    results = [
        adam_step(owned[slot], summed[slot], moments[slot], squares[slot], decays[slot])
        for slot in range(6)
    ]
    return (
        (layer_output, input_grad)
        + summed
        + tuple(result[0] for result in results)
        + tuple(result[1] for result in results)
        + tuple(result[2] for result in results)
    )


def solution(mesh):
    acts = P("fsdp", "seq", None)
    mat = P(("seq", "fsdp"), None)
    vec = P(("seq", "fsdp"))
    six = (mat, mat, mat, mat, vec, vec)
    return jax.shard_map(
        one_step,
        mesh=mesh,
        in_specs=(acts,) + six + (acts,) + (mat,) * 8 + (vec,) * 4,
        out_specs=(acts, acts) + six * 4,
        check_vma=False,
    )
```

```python
import functools
import jax
import jax.numpy as jnp
from jax import lax
from jax.experimental import pallas as pl
from jax.experimental.pallas import tpu as pltpu
from jax.sharding import PartitionSpec as P


F32 = jnp.float32
BF16 = jnp.bfloat16
EPS_NORM = 1e-05
HD = 64
ROT = 16
PAIR = 2 * HD
STEP = 10
BETA_ONE = 0.9
BETA_TWO = 0.95
RATE = 0.02
DECAY = 0.1
ADAM_EPS = 1e-08


def contract_last(left, right):
    return lax.dot_general(left, right, (((1,), (1,)), ((), ())), preferred_element_type=F32)


def contract_first(left, right):
    return lax.dot_general(left, right, (((0,), (0,)), ((), ())), preferred_element_type=F32)


def plain_dot(left, right):
    return lax.dot_general(left, right, (((1,), (0,)), ((), ())), preferred_element_type=F32)


def turn(pair_values, cosine, sine):
    lane = lax.broadcasted_iota(jnp.int32, (1, PAIR), 1)
    ahead = pltpu.roll(pair_values, PAIR - ROT // 2, 1)
    behind = pltpu.roll(pair_values, ROT // 2, 1)
    return pair_values * cosine + jnp.where(lane % HD < ROT // 2, -ahead, behind) * sine


def place(i, me, count):
    return ((i // count) ^ me[0]) * count + i % count


def piece_specs(pieces, block):
    count = pieces[0].shape[0] // block

    def spec(k):
        return pl.BlockSpec(
            (block, pieces[0].shape[1]), lambda i, me: (jnp.clip(i - k * count, 0, count - 1), 0)
        )

    return [spec(k) for k in range(len(pieces))]


def take_piece(refs, held, count):
    step = pl.program_id(0)
    for k, ref in enumerate(refs):

        @pl.when(step // count == k)
        def _():
            held[...] = ref[...]

    return held[...]


def normalize(rows, gain):
    centred = rows - jnp.mean(rows, axis=-1, keepdims=True)
    spread = jnp.mean(centred * centred, axis=-1, keepdims=True)
    return (centred * lax.rsqrt(spread + EPS_NORM) * gain).astype(BF16)


def project_kernel(count, me, x0, x1, x2, x3, ga_ref, w_ref, cos_ref, sin_ref, na_ref, qkv_ref, held):
    rows = take_piece((x0, x1, x2, x3), held, count).astype(F32)
    normed = normalize(rows, ga_ref[...])
    na_ref[...] = normed
    projected = plain_dot(normed, w_ref[...])
    width = w_ref.shape[1] // 3
    cosine = cos_ref[...]
    sine = sin_ref[...]
    for start in range(0, 3 * width, PAIR):
        columns = projected[:, start : start + PAIR]
        kind = start // PAIR % 3
        if kind < 2:
            columns = turn(columns, cosine, sine)
        columns = columns.astype(BF16)
        if kind == 0:
            columns = columns * jnp.asarray(HD**-0.5, BF16)
        qkv_ref[:, start : start + PAIR] = columns


def project(me, pieces, gain_attn, weight, tables, block=256):
    tokens, dim = pieces[0].shape
    count = tokens // block
    length = 4 * tokens
    width = weight.shape[1]
    whole = lambda i, me: (0, 0)
    part = lambda i, me: (place(i, me, count), 0)
    return pl.pallas_call(
        functools.partial(project_kernel, count),
        name="project",
        grid_spec=pltpu.PrefetchScalarGridSpec(
            num_scalar_prefetch=1,
            grid=(length // block,),
            in_specs=piece_specs(pieces, block)
            + [
                pl.BlockSpec((1, dim), whole),
                pl.BlockSpec((dim, width), whole),
                pl.BlockSpec((block, PAIR), part),
                pl.BlockSpec((block, PAIR), part),
            ],
            out_specs=[
                pl.BlockSpec((block, dim), part),
                pl.BlockSpec((block, width), part),
            ],
            scratch_shapes=[pltpu.VMEM((block, dim), BF16)],
        ),
        out_shape=[
            jax.ShapeDtypeStruct((length, dim), BF16),
            jax.ShapeDtypeStruct((length, width), BF16),
        ],
        cost_estimate=pl.CostEstimate(
            flops=2 * length * dim * width, bytes_accessed=6 * length * dim + 2 * length * width, transcendentals=0
        ),
    )(me, *pieces, gain_attn, weight, *tables)


def forward_kernel(block, q_ref, k_ref, v_ref, o_ref, lse_ref, v_first, v_second):
    at = pl.program_id(1)
    lane = lax.broadcasted_iota(jnp.int32, (1, PAIR), 1)
    first = lane < HD

    @pl.when(at == 0)
    def _():
        values = v_ref[...]
        one = jnp.ones_like(values)
        v_first[...] = jnp.where(first, values, one)
        v_second[...] = jnp.where(first, one, values)

    queries = q_ref[...]
    nil = jnp.zeros_like(queries)
    q_first = jnp.where(first, queries, nil)
    q_second = jnp.where(first, nil, queries)

    def one_head(q_part, v_part, start, masked, top, total):
        keys = k_ref[pl.ds(start, block), :]
        scores = contract_last(q_part, keys)
        if masked:
            row = lax.broadcasted_iota(jnp.int32, scores.shape, 0)
            col = lax.broadcasted_iota(jnp.int32, scores.shape, 1)
            scores = jnp.where(col <= row, scores, -1e30)
        new_top = jnp.maximum(top, jnp.max(scores, axis=-1, keepdims=True))
        weights = jnp.exp(scores - new_top).astype(BF16)
        total = total * jnp.exp(top - new_top) + plain_dot(weights, v_part[pl.ds(start, block), :])
        return new_top, total

    def both(j, state, masked):
        start = pl.multiple_of(j * block, block)
        top_a, sum_a, top_b, sum_b = state
        top_a, sum_a = one_head(q_first, v_first, start, masked, top_a, sum_a)
        top_b, sum_b = one_head(q_second, v_second, start, masked, top_b, sum_b)
        return top_a, sum_a, top_b, sum_b

    low = jnp.full((block, 1), -1e30, F32)
    zero = jnp.zeros((block, PAIR), F32)
    state = both(at, (low, zero, low, zero), True)
    state = lax.fori_loop(0, at, lambda j, s: both(j, s, False), state)
    top_a, sum_a, top_b, sum_b = state
    mixed = jnp.where(first, sum_a, sum_b)
    total = jnp.where(first, pltpu.roll(sum_a, HD, 1), pltpu.roll(sum_b, HD, 1))
    o_ref[...] = (mixed / total).astype(BF16)
    lse_ref[...] = jnp.where(first, top_a, top_b) + jnp.log(total)


def attend(qkv, block=512):
    length, width3 = qkv.shape
    width = width3 // 3
    pairs = width // PAIR
    steps = length // block
    return pl.pallas_call(
        functools.partial(forward_kernel, block),
        name="attend",
        grid=(pairs, steps),
        in_specs=[
            pl.BlockSpec((block, PAIR), lambda h, i: (i, 3 * h)),
            pl.BlockSpec((length, PAIR), lambda h, i: (0, 3 * h + 1)),
            pl.BlockSpec((length, PAIR), lambda h, i: (0, 3 * h + 2)),
        ],
        out_specs=[
            pl.BlockSpec((block, PAIR), lambda h, i: (i, h)),
            pl.BlockSpec((block, PAIR), lambda h, i: (i, h)),
        ],
        out_shape=[
            jax.ShapeDtypeStruct((length, width), BF16),
            jax.ShapeDtypeStruct((length, width), F32),
        ],
        scratch_shapes=[pltpu.VMEM((length, PAIR), BF16), pltpu.VMEM((length, PAIR), BF16)],
        cost_estimate=pl.CostEstimate(
            flops=8 * length * length * width, bytes_accessed=12 * length * width, transcendentals=length * length * width // HD
        ),
    )(qkv, qkv, qkv)


def backward_kernel(
    block, q_ref, k_ref, v_ref, o_ref, do_ref, lse_ref, cos_ref, sin_ref,
    grad_ref, q_a, q_b, k_a, k_b, do_a, do_b, top_row, dot_row, dq_sum,
):
    length = q_ref.shape[0]
    steps = length // block
    lane = lax.broadcasted_iota(jnp.int32, (1, PAIR), 1)
    first = lane < HD
    ones = jnp.ones((8, PAIR), BF16)
    for i in range(steps):
        at = pl.ds(i * block, block)
        nil = jnp.zeros((block, PAIR), BF16)
        for source, left, right in ((q_ref, q_a, q_b), (k_ref, k_a, k_b), (do_ref, do_a, do_b)):
            values = source[at, :]
            left[at, :] = jnp.where(first, values, nil)
            right[at, :] = jnp.where(first, nil, values)
        product = do_ref[at, :].astype(F32) * o_ref[at, :].astype(F32)
        high_part = product.astype(BF16)
        low_part = (product - high_part.astype(F32)).astype(BF16)
        for slot, keep in ((0, first), (1, jnp.logical_not(first))):
            dot_row[8 * slot : 8 * slot + 8, at] = contract_last(
                ones, jnp.where(keep, high_part, nil)
            ) + contract_last(ones, jnp.where(keep, low_part, nil))
        turned = jnp.transpose(lse_ref[at, :])
        top_row[0:8, at] = turned[0:8, :]
        top_row[8:16, at] = turned[HD : HD + 8, :]
    dq_sum[...] = jnp.zeros_like(dq_sum)

    def one_block(i, j, key_sum, value_sum, masked):
        q_at = pl.ds(pl.multiple_of(i * block, block), block)
        k_at = pl.ds(pl.multiple_of(j * block, block), block)
        keys = k_ref[k_at, :]
        values = v_ref[k_at, :]
        for slot, q_s, k_s, do_s in ((0, q_a, k_a, do_a), (1, q_b, k_b, do_b)):
            q_part = q_s[q_at, :]
            do_part = do_s[q_at, :]
            scores = contract_last(keys, q_part)
            if masked:
                key_at = lax.broadcasted_iota(jnp.int32, scores.shape, 0)
                query_at = lax.broadcasted_iota(jnp.int32, scores.shape, 1)
                scores = jnp.where(key_at <= query_at, scores, -1e30)
            soft = jnp.exp(scores - top_row[8 * slot : 8 * slot + 1, q_at])
            value_sum = value_sum + plain_dot(soft.astype(BF16), do_part)
            grad = contract_last(values, do_part)
            grad_scores = (soft * (grad - dot_row[8 * slot : 8 * slot + 1, q_at])).astype(BF16)
            key_sum = key_sum + plain_dot(grad_scores, q_part)
            dq_sum[q_at, :] += contract_first(grad_scores, k_s[k_at, :])
        return key_sum, value_sum

    def key_block(j, carry):
        zero = jnp.zeros((block, PAIR), F32)
        state = one_block(j, j, zero, zero, True)
        state = lax.fori_loop(j + 1, steps, lambda i, s: one_block(i, j, s[0], s[1], False), state)
        k_at = pl.ds(pl.multiple_of(j * block, block), block)
        grad_ref[k_at, PAIR : 2 * PAIR] = turn(state[0], cos_ref[k_at, :], -sin_ref[k_at, :]).astype(BF16)
        grad_ref[k_at, 2 * PAIR :] = state[1].astype(BF16)
        return carry

    lax.fori_loop(0, steps, key_block, 0)
    for i in range(steps):
        at = pl.ds(i * block, block)
        turned = turn(dq_sum[at, :] * HD**-0.5, cos_ref[at, :], -sin_ref[at, :])
        grad_ref[at, :PAIR] = turned.astype(BF16)


def attend_back(qkv, context, grad_context, lse, tables, pair, block=512):
    length = qkv.shape[0]
    col = lambda at: pl.BlockSpec((length, PAIR), lambda h: (0, at))
    whole = pl.BlockSpec((length, PAIR), lambda h: (0, 0))
    return pl.pallas_call(
        functools.partial(backward_kernel, block),
        name="attend_back",
        grid=(1,),
        in_specs=[col(3 * pair), col(3 * pair + 1), col(3 * pair + 2), col(pair), col(pair), col(pair), whole, whole],
        out_specs=pl.BlockSpec((length, 3 * PAIR), lambda h: (0, 0)),
        out_shape=jax.ShapeDtypeStruct((length, 3 * PAIR), BF16),
        scratch_shapes=[pltpu.VMEM((length, PAIR), BF16)] * 6
        + [pltpu.VMEM((16, length), F32)] * 2
        + [pltpu.VMEM((length, PAIR), F32)],
        cost_estimate=pl.CostEstimate(
            flops=20 * length * length * PAIR, bytes_accessed=20 * length * PAIR, transcendentals=2 * length * length
        ),
    )(qkv, qkv, qkv, context, grad_context, lse, *tables)


def unpack(up_ref, down_ref, up_held, down_held, fold_first):
    lead, second, rows, half = up_ref.shape
    fold, ways = (lead, second) if fold_first else (second, lead)
    for f in range(fold):
        for k in range(ways):
            source = (f, k) if fold_first else (k, f)
            at = (k * fold + f) * rows
            up_held[at : at + rows, :] = up_ref[source]
            at = (f * 2 + k % 2) * rows
            down_held[at : at + rows, (k // 2) * half : (k // 2 + 1) * half] = down_ref[source]


def packed_specs(packed):
    shape = (packed.shape[0], packed.shape[1], packed.shape[2] // 2, packed.shape[3])
    return [
        pl.BlockSpec(shape, lambda i, *_: (0, 0, 0, 0)),
        pl.BlockSpec(shape, lambda i, *_: (0, 0, 1, 0)),
    ]


def feed_core(normed, upstream, gain, down_ref, up_ref, act_ref, gh_ref):
    down = down_ref[...]
    up = up_ref[...]
    hidden = plain_dot(normed, up)
    back = contract_last(upstream, down)
    under = 0.5 + 0.5 * lax.erf(hidden * (0.5**0.5))
    activated = (hidden * under).astype(BF16)
    slope = under + hidden * jnp.exp(-0.5 * hidden * hidden) * 0.3989422804014327
    grad_hidden = (back * slope).astype(BF16)
    act_ref[...] = activated
    gh_ref[...] = grad_hidden
    return plain_dot(activated, down), contract_last(grad_hidden, up) * gain


def second_kernel(
    n_ref, g_ref, part_in, term_in, gain_ref, up_ref, down_ref,
    act_ref, gh_ref, part_ref, below_ref, up_held, down_held,
):
    @pl.when(pl.program_id(0) == 0)
    def _():
        unpack(up_ref, down_ref, up_held, down_held, False)

    part, term = feed_core(n_ref[...], g_ref[...], gain_ref[...], down_held, up_held, act_ref, gh_ref)
    part_ref[...] = (part + part_in[...].astype(F32)).astype(BF16)
    below_ref[...] = (term + term_in[...].astype(F32)).astype(BF16)


def mlp_second(normed, upstream, partial, term, gain_mlp, packed, block=256):
    length, dim = normed.shape
    hid = packed.shape[3]
    whole = lambda i: (0, 0)
    tile = lambda columns: pl.BlockSpec((block, columns), lambda i: (i, 0))
    shape = lambda columns: jax.ShapeDtypeStruct((length, columns), BF16)
    return pl.pallas_call(
        second_kernel,
        name="mlp_second",
        grid=(length // block,),
        in_specs=[
            tile(dim), tile(dim), tile(dim), tile(dim),
            pl.BlockSpec((1, dim), whole),
        ]
        + packed_specs(packed),
        out_specs=[tile(hid), tile(hid), tile(dim), tile(dim)],
        scratch_shapes=[pltpu.VMEM((dim, hid), BF16), pltpu.VMEM((hid, dim), BF16)],
        out_shape=[shape(hid), shape(hid), shape(dim), shape(dim)],
        cost_estimate=pl.CostEstimate(
            flops=8 * length * dim * hid, bytes_accessed=16 * length * dim + 4 * dim * hid, transcendentals=2 * length * hid
        ),
    )(normed, upstream, partial, term, gain_mlp, packed, packed)


def mlp_kernel(
    count, me, x0, x1, x2, x3, g0, g1, g2, g3, gain_ref, up_ref, down_ref,
    n_ref, act_ref, gh_ref, g_ref, part_ref, below_ref, x_held, g_held, up_held, down_held,
):
    @pl.when(pl.program_id(0) == 0)
    def _():
        unpack(up_ref, down_ref, up_held, down_held, True)

    gain = gain_ref[...]
    normed = normalize(take_piece((x0, x1, x2, x3), x_held, count).astype(F32), gain)
    n_ref[...] = normed
    upstream = take_piece((g0, g1, g2, g3), g_held, count)
    g_ref[...] = upstream
    part, term = feed_core(normed, upstream, gain, down_held, up_held, act_ref, gh_ref)
    part_ref[...] = part.astype(BF16)
    below_ref[...] = term.astype(BF16)


def mlp(me, pieces, grad_pieces, gain_mlp, packed, block=256):
    tokens, dim = pieces[0].shape
    length = 4 * tokens
    hid = packed.shape[3]
    count = tokens // block
    whole = lambda i, me: (0, 0)
    part = lambda i, me: (place(i, me, count), 0)
    tile = lambda columns: pl.BlockSpec((block, columns), part)
    shape = lambda columns: jax.ShapeDtypeStruct((length, columns), BF16)
    return pl.pallas_call(
        functools.partial(mlp_kernel, count),
        name="mlp",
        grid_spec=pltpu.PrefetchScalarGridSpec(
            num_scalar_prefetch=1,
            grid=(length // block,),
            in_specs=piece_specs(pieces, block)
            + piece_specs(grad_pieces, block)
            + [
                pl.BlockSpec((1, dim), whole),
            ]
            + packed_specs(packed),
            out_specs=[tile(dim), tile(hid), tile(hid), tile(dim), tile(dim), tile(dim)],
            scratch_shapes=[
                pltpu.VMEM((block, dim), BF16),
                pltpu.VMEM((block, dim), BF16),
                pltpu.VMEM((dim, hid), BF16),
                pltpu.VMEM((hid, dim), BF16),
            ],
        ),
        out_shape=[shape(dim), shape(hid), shape(hid), shape(dim), shape(dim), shape(dim)],
        cost_estimate=pl.CostEstimate(
            flops=8 * length * dim * hid, bytes_accessed=16 * length * dim + 4 * dim * hid, transcendentals=2 * length * hid
        ),
    )(me, *pieces, *grad_pieces, gain_mlp, packed, packed)


def below_kernel(me, first_ref, second_ref, w_ref, gain_ref, term_ref, o_ref):
    grad = contract_last(jnp.concatenate([first_ref[...], second_ref[...]], axis=1), w_ref[...])
    o_ref[...] = (grad * gain_ref[...] + term_ref[...].astype(F32)).astype(BF16)


def below(me, flip, first, second, weight, gain, term):
    length, half = first.shape
    block = length // 4
    dim = weight.shape[0]
    part = lambda i, me: (2 * i + ((me[0] & 1) ^ flip), 0)
    whole = lambda i, me: (0, 0)
    return pl.pallas_call(
        below_kernel,
        name="below",
        grid_spec=pltpu.PrefetchScalarGridSpec(
            num_scalar_prefetch=1,
            grid=(2,),
            in_specs=[
                pl.BlockSpec((block, half), part),
                pl.BlockSpec((block, half), part),
                pl.BlockSpec((dim, 2 * half), whole),
                pl.BlockSpec((1, dim), whole),
                pl.BlockSpec((block, dim), part),
            ],
            out_specs=pl.BlockSpec((block, dim), lambda i, me: (i, 0)),
        ),
        out_shape=jax.ShapeDtypeStruct((2 * block, dim), BF16),
        cost_estimate=pl.CostEstimate(
            flops=2 * length * dim * half, bytes_accessed=2 * length * dim + 2 * length * half, transcendentals=0
        ),
    )(me, first, second, weight, gain, term)


def swap(values, axis, bit):
    ways = lax.axis_size(axis)
    return lax.ppermute(values, axis, [(i, i ^ bit) for i in range(ways)])


def bits_of(ways):
    return [1 << k for k in range(ways.bit_length() - 1)]


def bit_set(axis, bit):
    return (lax.axis_index(axis) & bit) != 0


def pick(values, at, axis):
    return lax.dynamic_index_in_dim(values, at, axis, keepdims=False)


def gather_far_first(shard, axis, at):
    held = shard
    for bit in reversed(bits_of(lax.axis_size(axis))):
        other = swap(held, axis, bit)
        upper = bit_set(axis, bit)
        held = jnp.stack([jnp.where(upper, other, held), jnp.where(upper, held, other)], axis=at)
        at += 1
    return held


def reduce_near_first(values, axis, at):
    bits = bits_of(lax.axis_size(axis))
    held = values.reshape(values.shape[:at] + (2,) * len(bits) + values.shape[at + 1 :])
    for bit in bits:
        mine = (lax.axis_index(axis) & bit) // bit
        spot = at + len(bits) - bits.index(bit) - 1
        arrived = swap(pick(held, 1 - mine, spot), axis, bit)
        held = (pick(held, mine, spot).astype(F32) + arrived.astype(F32)).astype(BF16)
    return held


def exchange(values, axis):
    ways = lax.axis_size(axis)
    me = lax.axis_index(axis)
    pieces = [pick(values, me, 0)]
    for k in range(1, ways):
        pieces.append(swap(pick(values, me ^ k, 0), axis, k))
    count = len(bits_of(ways))
    held = jnp.stack(pieces).reshape((2,) * count + pieces[0].shape)
    for spot, bit in enumerate(reversed(bits_of(ways))):
        held = jnp.where(bit_set(axis, bit), jnp.flip(held, spot), held)
    return held.reshape((ways,) + pieces[0].shape)


def gather_sequence(rows):
    near = swap(rows, "seq", 1)
    far = swap(rows, "seq", 2)
    return rows, near, far, swap(far, "seq", 1)


def sum_sequence(partial):
    me = lax.axis_index("seq")
    tokens = partial.shape[0] // 4
    held = partial.reshape(2, 2, tokens, partial.shape[1])
    mine = me & 1
    arrived = swap(pick(held, 1 - mine, 1), "seq", 1)
    held = (pick(held, mine, 1).astype(F32) + arrived.astype(F32)).astype(BF16)
    mine = me >> 1
    arrived = swap(pick(held, 1 - mine, 0), "seq", 2)
    return pick(held, mine, 0).astype(F32) + arrived.astype(F32)


def rotary_tables(length):
    lane = jnp.arange(PAIR, dtype=jnp.int32) % HD
    step = (lane % (ROT // 2)).astype(F32)
    frequency = jnp.where(lane < ROT, 10000.0 ** (-(step * 2.0) / ROT), 0.0)
    angles = jnp.arange(length, dtype=jnp.int32).astype(F32)[:, None] * frequency[None, :]
    return jnp.cos(angles), jnp.sin(angles)


def adam_step(weight, gradient, moment, square, decay_rate):
    moment_next = BETA_ONE * moment + (1.0 - BETA_ONE) * gradient
    square_next = BETA_TWO * square + (1.0 - BETA_TWO) * gradient * gradient
    moment_hat = moment_next / (1.0 - BETA_ONE**STEP)
    square_hat = square_next / (1.0 - BETA_TWO**STEP)
    change = -RATE * (
        moment_hat / (jnp.sqrt(square_hat) + ADAM_EPS) + decay_rate * weight.astype(F32)
    )
    return (moment_next, square_next, change)


def one_step(
    layer_input, w_qkv, w_out, w_up, w_down, gain_attn, gain_mlp, out_grad,
    moment_qkv, square_qkv, moment_out, square_out, moment_up, square_up, moment_down, square_down,
    moment_gattn, square_gattn, moment_gmlp, square_gmlp,
):
    ways = lax.axis_size("seq")
    fold = lax.axis_size("fsdp")
    rows = w_qkv.shape[0]
    dim = rows * ways * fold
    inner = w_qkv.shape[1] // 3
    group = inner // ways
    hid = w_up.shape[1] // ways
    tokens = layer_input.shape[1]
    length = tokens * ways

    me = lax.axis_index("seq").astype(jnp.int32).reshape(1)
    gains = gather_far_first(
        gather_far_first(jnp.stack([gain_attn, gain_mlp]), "seq", 1), "fsdp", 3
    ).reshape(2, dim).astype(F32)
    down_rows = w_down.shape[0]
    half_rows = down_rows // 2
    half = hid // 2
    split_up = (
        w_up.reshape(rows, ways, fold, 2, half_rows).transpose(1, 3, 0, 2, 4).reshape(ways, 2, rows, half)
    )
    local_up = exchange(split_up, "seq")
    local_down = (
        w_down.reshape(2, 2, rows, 2, half).transpose(0, 3, 1, 2, 4).reshape(2, ways, rows, half)
    )
    packed = [jnp.concatenate([local_up[:, k], local_down[k]], axis=1) for k in range(2)]
    first = lax.all_gather(packed[0], "fsdp")
    second = gather_far_first(packed[1], "fsdp", 1).reshape(ways, fold, 2 * rows, half)

    local_rows = layer_input[0]
    row_pieces = gather_sequence(local_rows)
    grad_pieces = gather_sequence(out_grad[0])
    count = group // PAIR
    split_qkv = (
        w_qkv.reshape(rows, 3, ways, count, PAIR).transpose(2, 0, 3, 1, 4).reshape(ways, rows, 3 * group)
    )
    local_qkv = exchange(split_qkv, "seq")
    flat_out = w_out.reshape(rows, ways, dim // ways).transpose(1, 0, 2)
    both = lax.all_gather(jnp.concatenate([local_qkv, flat_out], axis=2), "fsdp")
    full_qkv = both[..., : 3 * group].transpose(1, 0, 2, 3).reshape(dim, 3 * group)
    full_out = both[..., 3 * group :].transpose(0, 2, 1, 3).reshape(fold * rows, dim)
    tables = rotary_tables(length)
    gains, tables = lax.optimization_barrier((gains, tables))

    normed_mlp, activated, grad_hidden, upstream, partial, mlp_term = mlp(
        me, row_pieces, grad_pieces, gains[1:2], first
    )

    def feed_gradients(activated, grad_hidden):
        grad_wdown = contract_first(activated, upstream).astype(BF16)
        grad_wup = contract_first(normed_mlp, grad_hidden).astype(BF16)
        return (
            grad_wdown.reshape(fold, half_rows, dim),
            grad_wup.reshape(ways, fold, rows, half).transpose(1, 0, 2, 3).reshape(fold, ways * rows, half),
        )

    grads_first = feed_gradients(activated, grad_hidden)
    grads_first, partial = lax.optimization_barrier((grads_first, partial))
    activated, grad_hidden, partial, mlp_term = mlp_second(
        normed_mlp, upstream, partial, mlp_term, gains[1:2], second
    )
    grads_second = feed_gradients(activated, grad_hidden)
    sendable = jnp.concatenate(
        [grads_first[0], grads_second[0], jnp.concatenate([grads_first[1], grads_second[1]], axis=2)], axis=1
    )
    sendable, full_qkv = lax.optimization_barrier((sendable, full_qkv))
    owned_sum = lax.psum_scatter(sendable, "fsdp", scatter_dimension=0)

    normed_attn, qkv = project(me, row_pieces, gains[0:1], full_qkv, tables)
    context, lse = attend(qkv)
    grad_context = contract_last(upstream, full_out).astype(BF16)
    partial = (plain_dot(context, full_out) + partial.astype(F32)).astype(BF16)
    grad_wout = contract_first(context, upstream).astype(BF16)
    grad_context, partial, grad_wout = lax.optimization_barrier((grad_context, partial, grad_wout))
    branch = sum_sequence(partial)
    layer_output = (local_rows.astype(F32) + branch).astype(BF16)[None]
    sum_out = reduce_near_first(grad_wout.reshape(fold, rows, dim), "fsdp", 0).astype(F32)

    near_pairs = []
    grad_pairs = []
    for pair in range(count):
        grad_pair = attend_back(qkv, context, grad_context, lse, tables, pair)
        grad_pairs.append(grad_pair)
        if pair + 1 == count:
            sent = below(me, 1, *grad_pairs, full_qkv, gains[0:1], mlp_term)
            grad_pair, sent = lax.optimization_barrier((grad_pair, sent))
        grad_weight = contract_first(normed_attn, grad_pair).astype(BF16)
        if pair + 1 < count:
            grad_weight, grad_context = lax.optimization_barrier((grad_weight, grad_context))
        near = reduce_near_first(grad_weight.reshape(ways, fold, rows, 3 * PAIR), "fsdp", 1)
        near_pairs.append(near)
    arrived = swap(sent, "seq", 1)
    kept = below(me, 0, *grad_pairs, full_qkv, gains[0:1], mlp_term)
    held = (kept.astype(F32) + arrived.astype(F32)).astype(BF16).reshape(2, tokens, dim)
    mine = lax.axis_index("seq") >> 1
    outward = pick(held, 1 - mine, 0)
    inward = jnp.concatenate([swap(outward[: tokens // 2], "seq", 2), swap(outward[tokens // 2 :], "seq", 2)])
    upper = pick(held, mine, 0).astype(F32) + inward.astype(F32)
    sum_down = owned_sum[:down_rows].astype(F32)
    back_up = exchange(owned_sum[down_rows:].reshape(ways, rows, hid), "seq")
    sum_up = (
        back_up.reshape(ways, rows, 2, fold, half_rows).transpose(1, 0, 3, 2, 4).reshape(rows, ways * hid).astype(F32)
    )
    near_qkv = jnp.concatenate(near_pairs, axis=2)
    back_qkv = exchange(near_qkv, "seq")
    sum_qkv = (
        back_qkv.reshape(ways, rows, count, 3, PAIR).transpose(1, 3, 0, 2, 4).reshape(rows, 3 * inner).astype(F32)
    )

    local = local_rows.astype(F32)
    centred = local - jnp.mean(local, axis=-1, keepdims=True)
    inverse = lax.rsqrt(jnp.mean(centred * centred, axis=-1, keepdims=True) + EPS_NORM)
    xhat = centred * inverse
    term = inverse * (
        upper
        - jnp.mean(upper, axis=-1, keepdims=True)
        - xhat * jnp.mean(upper * xhat, axis=-1, keepdims=True)
    )
    input_grad = (out_grad[0].astype(F32) + term).astype(BF16)[None]

    sum_gattn = jnp.sum(w_qkv.astype(F32) * sum_qkv, axis=1) / gain_attn.astype(F32)
    sum_gmlp = jnp.sum(w_up.astype(F32) * sum_up, axis=1) / gain_mlp.astype(F32)
    summed = (sum_qkv, sum_out, sum_up, sum_down, sum_gattn, sum_gmlp)
    owned = (w_qkv, w_out, w_up, w_down, gain_attn, gain_mlp)
    moments = (moment_qkv, moment_out, moment_up, moment_down, moment_gattn, moment_gmlp)
    squares = (square_qkv, square_out, square_up, square_down, square_gattn, square_gmlp)
    decays = (DECAY, DECAY, DECAY, DECAY, 0.0, 0.0)
    results = [
        adam_step(owned[slot], summed[slot], moments[slot], squares[slot], decays[slot])
        for slot in range(6)
    ]
    return (
        (layer_output, input_grad)
        + summed
        + tuple(result[0] for result in results)
        + tuple(result[1] for result in results)
        + tuple(result[2] for result in results)
    )


def solution(mesh):
    acts = P("fsdp", "seq", None)
    mat = P(("seq", "fsdp"), None)
    vec = P(("seq", "fsdp"))
    six = (mat, mat, mat, mat, vec, vec)
    return jax.shard_map(
        one_step,
        mesh=mesh,
        in_specs=(acts,) + six + (acts,) + (mat,) * 8 + (vec,) * 4,
        out_specs=(acts, acts) + six * 4,
        check_vma=False,
    )
```
